32 devices in a mesh: parts: 2 (over x), row: 8 (over z, y), col: 2 (over core).
Axes of the slice: x: 2, y: 2, z: 4, core: 2. Of those that a mesh axis runs over, the one named last changes fastest.
Arguments:
- spectra: bfloat16 [4, 32, 2, 32, 1024], P('parts', None, None, ('row', 'col')), parts along dimension 0, may hold values from -6 to 6
- window_flags: int32 [64, 32], P('parts', ('row', 'col')), parts along dimension 0, may hold values 0 or 1
Outputs:
- cross: float32 [4, 2, 2, 16, 32, 1024], P('parts', None, 'col', None, 'row'), parts along dimension 0
The draws below stay inside these ranges and needn't reach their ends.
There are 2 independent parts, one for each index of `parts`. The reference program is written for one: setup_inputs(seed, part) draws one part's arguments, and reference() takes and returns one part's arrays. A program takes and returns all parts, laid end to end along the dimension named above; each array names one. Nothing has to cross between parts.
All inputs are finite; a program needn't handle non-finite values. No bound on the sum of `window_flags` on one device may be relied on, other than what follows from the above.
Results may differ from the reference program's by a relative error of at most 0.0034.
Values may be sent and summed in bfloat16 or wider, within the bound.
A program may use at most 256 MiB of HBM per device.

```python
import jax
import jax.numpy as jnp

CH_DEV = 2
W = 32
BANDS = 2
FB = 1024
HALFWIN = 64
C = 32
N_ROW = 8
N_COL = 2


def plant(entries, stream_key, least, largest):
    extent = entries.shape
    spot = [jax.random.randint(jax.random.fold_in(stream_key, axis), (), 0, extent[axis]) for axis in range(len(extent))]
    entries = entries.at[tuple(spot)].set(least)
    longest = extent.index(max(extent))
    spot[longest] = (spot[longest] + 1) % extent[longest]
    return entries.at[tuple(spot)].set(largest)


def block_levels(own_key, shape, cuts, least, top_value):
    gain, own = 1.0, jax.random.fold_in(own_key, 6)
    for axis_at, blocks in cuts:
        draws = jnp.exp(jax.random.uniform(jax.random.fold_in(own, axis_at), (blocks,), jnp.float32, least / len(cuts), top_value / len(cuts)))
        gain = gain * jnp.repeat(draws, shape[axis_at] // blocks).reshape([-1 if axis == axis_at else 1 for axis in range(len(shape))])
    return gain


def centred(key, extent, spread, bound, pieces=(), kind=jnp.bfloat16):
    drawn = jax.random.normal(key, extent, jnp.float32) * spread
    if len(pieces) > 0:
        drawn = block_levels(key, extent, pieces, -0.22, 0.18) * drawn
    return jnp.clip(drawn, min=-bound, max=bound).astype(kind)


def setup_inputs(seed: int = 0, part: int = 0) -> dict:
    key_of = jax.random.split(jax.random.key(seed), 3)
    own_keys = jax.random.split(jax.random.fold_in(key_of[2], part), 3)
    return {
        "spectra": centred(own_keys[0], (BANDS, W, 2, C, FB), 1.0, 6.0, ((3, 16),)),
        "window_flags": plant((jax.random.randint(own_keys[1], (W, C), 0, 4) < 3).astype(jnp.int32), jax.random.fold_in(own_keys[1], 1), 0, 1),
    }


epsilon = 1e-06

def window_mean(magnitude):
    bins = magnitude.shape[-1]
    lead = [(0, 0)] * (magnitude.ndim - 1)
    padded = jnp.pad(magnitude, lead + [(HALFWIN + 1, HALFWIN)])
    running = jnp.cumsum(padded, axis=-1)
    total = running[..., 2 * HALFWIN + 1:] - running[..., :bins]
    positions = jnp.arange(bins, dtype=jnp.int32)
    counted = (jnp.minimum(positions + HALFWIN, bins - 1) - jnp.maximum(positions - HALFWIN, 0) + 1).astype(jnp.float32)
    return total / counted

def whiten(values):
    magnitude = jnp.sqrt(values[:, :, 0] * values[:, :, 0] + values[:, :, 1] * values[:, :, 1])
    smooth = window_mean(magnitude)
    return (values / (smooth[:, :, None] + epsilon)).astype(jnp.bfloat16)

def reference(spectra, window_flags):
    flagged = spectra.astype(jnp.float32) * window_flags.astype(jnp.float32)[None, :, None, :, None]
    whitened = whiten(flagged)
    grouped = whitened.reshape(BANDS, W, 2, N_ROW, N_COL, CH_DEV, FB)
    total = N_ROW * N_COL * CH_DEV
    half_size = total // N_COL
    second = jnp.arange(total, dtype=jnp.int32)
    results = []
    for band_index in range(BANDS):
        halves = []
        for half_index in range(N_COL):
            first_rows = grouped[band_index, :, :, :, half_index].reshape(W, 2, half_size, FB).astype(jnp.float32)
            all_rows = whitened[band_index].astype(jnp.float32)
            prods = jnp.einsum('wpif,wqjf->pqijf', first_rows, all_rows)
            real_part = prods[0, 0] + prods[1, 1]
            imag_part = prods[1, 0] - prods[0, 1]
            slot = jnp.arange(half_size, dtype=jnp.int32)
            first = (slot // CH_DEV * N_COL + half_index) * CH_DEV + slot % CH_DEV
            keep = (first[:, None] <= second[None, :]).astype(jnp.float32)[:, :, None]
            halves.append(jnp.stack([real_part * keep, imag_part * keep], axis=0))
        results.append(jnp.stack(halves, axis=1))
    return jnp.stack(results, axis=0)
```

```python
import functools

import jax
import jax.numpy as jnp
from jax import lax
from jax.experimental import pallas as pl
from jax.experimental.pallas import tpu as pltpu
from jax.sharding import PartitionSpec as P

HALFWIN = 64
LANES = 128
epsilon = 1e-06


def window_mean(magnitude):
    bins = magnitude.shape[-1]
    positions = jnp.arange(bins, dtype=jnp.int32)
    near = (jnp.abs(positions[:, None] - positions[None, :]) <= HALFWIN).astype(jnp.float32)
    total = jnp.einsum("...g,gf->...f", magnitude, near, precision=lax.Precision.HIGHEST)
    counted = (
        jnp.minimum(positions + HALFWIN, bins - 1) - jnp.maximum(positions - HALFWIN, 0) + 1
    ).astype(jnp.float32)
    return total / counted


def whiten(values):
    magnitude = jnp.sqrt(values[:, :, 0] * values[:, :, 0] + values[:, :, 1] * values[:, :, 1])
    smooth = window_mean(magnitude)
    return (values / (smooth[:, :, None] + epsilon)).astype(jnp.bfloat16)


def combine_parts(prods, keep):
    real_part = prods[..., 0, 0, :, :, :] + prods[..., 1, 1, :, :, :]
    imag_part = prods[..., 1, 0, :, :, :] - prods[..., 0, 1, :, :, :]
    return jnp.stack([real_part * keep, imag_part * keep], axis=-4)


def gather_form(spectra, window_flags):
    per_device = spectra.shape[3]
    flag_values = window_flags.astype(jnp.float32)[None, :, None, :, None]
    payload = whiten(spectra.astype(jnp.float32) * flag_values)
    row_index = lax.axis_index("row")
    col_index = lax.axis_index("col")
    col_count = lax.axis_size("col")
    row_count = lax.axis_size("row")
    half_size = row_count * per_device
    cols_here = col_count * per_device
    slot = jnp.arange(half_size, dtype=jnp.int32)
    first = (slot // per_device * col_count + col_index) * per_device + slot % per_device
    second = row_index * cols_here + jnp.arange(cols_here, dtype=jnp.int32)
    keep = (first[:, None] <= second[None, :]).astype(jnp.float32)[:, :, None]
    pieces = []
    for band_index in range(spectra.shape[0]):
        first_rows = lax.all_gather(payload[band_index : band_index + 1], "row", axis=3, tiled=True)
        second_rows = lax.all_gather(
            payload[band_index : band_index + 1], "col", axis=3, tiled=True
        )
        prods = jnp.einsum(
            "wpif,wqjf->pqijf", first_rows[0], second_rows[0], preferred_element_type=jnp.float32
        )
        pieces.append(combine_parts(prods, keep))
    result = jnp.stack(pieces, axis=0)
    return result[:, :, None]


def spread_band(x_ref, flag_ref, rows_ref, b):
    _, windows, parts, chans, _ = x_ref.shape
    for w in range(windows):
        for p in range(parts):
            pair = x_ref[b, w, p].astype(jnp.float32)
            for n in range(rows_ref.shape[1]):
                rows_ref[p, n, pl.ds(w * chans, chans)] = pair[:, n * LANES : (n + 1) * LANES]
    extent = (windows, windows)
    same = lax.broadcasted_iota(jnp.int32, extent, 0) == lax.broadcasted_iota(jnp.int32, extent, 1)
    flags = flag_ref[...].astype(jnp.float32)
    return [
        jnp.sum(jnp.where(same, flags[c : c + 1], 0.0), axis=1, keepdims=True)
        for c in range(chans)
    ]


def whiten_band(x_ref, flag_ref, rows_ref, y_ref, b):
    _, windows, _, chans, bins = x_ref.shape
    flags = spread_band(x_ref, flag_ref, rows_ref, b)
    step = 2 * LANES
    chunks = bins // LANES
    near = lax.broadcasted_iota(jnp.int32, (2 * step, step), 0) - LANES
    here = lax.broadcasted_iota(jnp.int32, (2 * step, step), 1)
    inside = (jnp.abs(near - here) <= HALFWIN).astype(jnp.float32).astype(jnp.bfloat16)
    mags = []
    for c in range(chans):
        picked = pl.ds(c, windows, stride=chans)
        line = []
        for n in range(chunks):
            re = rows_ref[0, n, picked] * flags[c]
            im = rows_ref[1, n, picked] * flags[c]
            line.append(jnp.sqrt(re * re + im * im))
        mags.append(jnp.concatenate(line, axis=1))
    mag = jnp.concatenate(mags, axis=0)
    high = mag.astype(jnp.bfloat16)
    low = (mag - high.astype(jnp.float32)).astype(jnp.bfloat16)
    for at in range(0, bins, step):
        start, stop = max(at - LANES, 0), min(at + step + LANES, bins)
        near_rows = inside[start - at + LANES : stop - at + LANES]
        total = jnp.dot(
            high[:, start:stop], near_rows, preferred_element_type=jnp.float32
        ) + jnp.dot(low[:, start:stop], near_rows, preferred_element_type=jnp.float32)
        spot = at + lax.broadcasted_iota(jnp.int32, (1, step), 1)
        counted = (
            jnp.minimum(spot + HALFWIN, bins - 1) - jnp.maximum(spot - HALFWIN, 0) + 1
        ).astype(jnp.float32)
        scale = 1.0 / (total / counted + epsilon)
        for c in range(chans):
            picked = pl.ds(c, windows, stride=chans)
            for p in range(2):
                for half in range(2):
                    lanes = slice(half * LANES, (half + 1) * LANES)
                    value = rows_ref[p, at // LANES + half, picked] * flags[c]
                    out = value * scale[c * windows : (c + 1) * windows, lanes]
                    y_ref[
                        b, at // LANES + half, pl.ds((c * 2 + p) * windows, windows)
                    ] = out.astype(jnp.bfloat16)


def fold(values):
    index = lax.broadcasted_iota(jnp.int32, values[0].shape, 0)
    shift = 1
    while len(values) > 1:
        even = lax.rem(index // shift, 2) == 0
        paired = []
        for n in range(0, len(values), 2):
            u, v = values[n], values[n + 1]
            moved = pltpu.roll(jnp.where(even, v, u), 8 - shift, 0)
            paired.append(jnp.where(even, u, v) + moved)
        values = paired
        shift *= 2
    return values[0]


def by_eight(values):
    total = values[0:8]
    for at in range(8, values.shape[0], 8):
        total = total + values[at : at + 8]
    return total


def block(wide_ref, first, second, cols):
    out = []
    for h in range(cols):
        reals, imags = [], []
        for k in range(2):
            re_a, im_a = wide_ref[first + h * 2 + k, 0], wide_ref[first + h * 2 + k, 1]
            for n in range(cols * 2):
                re_j, im_j = wide_ref[second + n, 0], wide_ref[second + n, 1]
                reals.append(by_eight(re_a * re_j + im_a * im_j))
                imags.append(by_eight(im_a * re_j - re_a * im_j))
        out.append(jnp.concatenate([fold(reals), fold(imags)], axis=0).astype(jnp.bfloat16))
    return out


def main_kernel(
    rows, cols, raw_ref, flag_ref, got_ref, x_ref, spread, sent, held, near_held, wide, near_wide,
    far_pairs, near_pairs, here_sem, in_sem, far_send, far_recv, near_send, near_recv, own_sem,
    cross_send, cross_recv, cross_own, same_send, same_recv, same_own,
):
    count, half_rows = rows * cols, rows // 2
    places = half_rows * cols
    per_row = cols * 2
    windows = x_ref.shape[1]
    row, col = lax.axis_index("row"), lax.axis_index("col")
    me = row * cols + col
    side, line = row // half_rows, lax.rem(row, half_rows)
    spot = line * cols + col
    other = 1 - side

    def remote(src, dst, send_sem, recv_sem, to_row, to_col):
        return pltpu.make_async_remote_copy(
            src_ref=src,
            dst_ref=dst,
            send_sem=send_sem,
            recv_sem=recv_sem,
            device_id={"row": to_row, "col": to_col},
            device_id_type=pl.DeviceIdType.MESH,
        )

    def signal(sem, peer):
        pl.semaphore_signal(
            sem,
            inc=1,
            device_id={"row": peer // cols, "col": lax.rem(peer, cols)},
            device_id_type=pl.DeviceIdType.MESH,
        )

    loads = []
    for n, b in enumerate((other, side)):
        loads.append(pltpu.make_async_copy(raw_ref.at[b], x_ref.at[b], in_sem.at[n]))
        loads[n].start()
    barrier = pltpu.get_barrier_semaphore()
    for k in range(1, count):
        peer = lax.rem(me + k, count)

        @pl.when(peer // cols >= row)
        def _():
            signal(barrier, peer)

    pl.semaphore_wait(barrier, row * cols + cols - 1)
    for k in range(1, count):
        peer = lax.rem(me + k, count)

        @pl.when(peer // cols < row)
        def _():
            signal(here_sem.at[row], peer)

    def ready(to_row):
        @pl.when(to_row > row)
        def _():
            pl.semaphore_wait(here_sem.at[to_row], cols)

    def far_copy(to_line, to_col):
        to = to_line * cols + to_col
        return remote(
            sent.at[other, to], held.at[me], far_send.at[other * places + to], far_recv.at[me],
            other * half_rows + to_line, to_col,
        )

    def main_copy(to_line, to_col):
        to = to_line * cols + to_col
        return remote(
            sent.at[side, to], held.at[me], far_send.at[side * places + to], far_recv.at[me],
            side * half_rows + to_line, to_col,
        )

    def near_copy(to_line, to_col):
        to = to_line * cols + to_col
        return remote(
            sent.at[other, to], near_held.at[spot], near_send.at[to], near_recv.at[spot],
            side * half_rows + to_line, to_col,
        )

    owns = [
        pltpu.make_async_copy(sent.at[side, spot], held.at[me], own_sem.at[0]),
        pltpu.make_async_copy(sent.at[other, spot], near_held.at[spot], own_sem.at[1]),
    ]
    loads[0].wait()
    whiten_band(x_ref, flag_ref, spread, sent, other)
    far_order = [
        (2 * (i // 2) + lax.rem(row + i, 2), lax.rem(col + j, cols))
        for i in range(half_rows)
        for j in range(cols)
    ]
    near_order = [
        (lax.rem(line + i, half_rows), lax.rem(col + j, cols))
        for i in range(half_rows)
        for j in range(cols)
    ][1:]
    for n, (to_line, to_col) in enumerate(far_order):
        if n % cols == 0:
            ready(other * half_rows + to_line)
        far_copy(to_line, to_col).start()
    loads[1].wait()
    whiten_band(x_ref, flag_ref, spread, sent, side)
    for n, (to_line, to_col) in enumerate(near_order):
        if n % cols == cols - 1:
            ready(side * half_rows + to_line)
        main_copy(to_line, to_col).start()
    for own in owns:
        own.start()
    for to_line, to_col in near_order:
        near_copy(to_line, to_col).start()

    def widen(slot, wide_ref, base):
        for c in range(2):
            for p in range(2):
                wide_ref[base + c, p] = slot[pl.ds((c * 2 + p) * windows, windows)].astype(
                    jnp.float32
                )

    def take(n):
        remote(sent.at[0, 0], held.at[n], far_send.at[0], far_recv.at[n], row, col).wait_recv()
        widen(held.at[n], wide, n * 2)

    def same_copy(kind, chunk, k, h):
        to = k * cols + h
        return remote(
            near_pairs.at[kind, to, pl.ds(0, k + 1)], got_ref.at[1, chunk, pl.ds(0, k + 1)],
            same_send.at[kind, to], same_recv.at[chunk], side * half_rows + k, h,
        )

    def same_local(kind, chunk, k, h):
        to = k * cols + h
        return pltpu.make_async_copy(
            near_pairs.at[kind, to, pl.ds(0, k + 1)], got_ref.at[1, chunk, pl.ds(0, k + 1)],
            same_own.at[kind],
        )

    def same(kind, wide_ref, base):
        chunk = (side if kind == 0 else other) * places + spot

        @pl.loop(0, half_rows)
        def _(step):
            r = lax.rem(line + 1 + step, half_rows)

            @pl.loop(0, r + 1)
            def _(q):
                found = block(wide_ref, base + q * per_row, base + r * per_row, cols)
                for h in range(cols):
                    near_pairs[kind, r * cols + h, q] = found[h]

            for k in range(half_rows):

                @pl.when(r == k)
                def _():
                    for h in range(cols):

                        @pl.when(spot != k * cols + h)
                        def _():
                            same_copy(kind, chunk, k, h).start()

                        @pl.when(spot == k * cols + h)
                        def _():
                            same_local(kind, chunk, k, h).start()

    owns[0].wait()
    widen(held.at[me], wide, me * 2)

    @pl.loop(1, places)
    def _(n):
        take(side * places + lax.rem(spot + n, places))

    same(0, wide, side * half_rows * per_row)

    owns[1].wait()
    widen(near_held.at[spot], near_wide, spot * 2)

    @pl.loop(1, places)
    def _(n):
        at = lax.rem(spot + n, places)
        remote(
            sent.at[0, 0], near_held.at[at], near_send.at[0], near_recv.at[at], row, col
        ).wait_recv()
        widen(near_held.at[at], near_wide, at * 2)

    same(1, near_wide, 0)

    @pl.loop(0, places)
    def _(n):
        take(other * places + n)

    def cross_copy(r, h):
        return remote(
            far_pairs.at[r * cols + h], got_ref.at[0, me], cross_send.at[r * cols + h],
            cross_recv.at[me], half_rows + r, h,
        )

    def cross_local(r, h):
        return pltpu.make_async_copy(far_pairs.at[r * cols + h], got_ref.at[0, me], cross_own)

    @pl.loop(0, half_rows)
    def _(step):
        pair = lax.rem(step // 2 + half_rows // 2 - 1, half_rows // 2)
        r = pair * 2 + lax.rem(step + row, 2)

        @pl.loop(0, half_rows)
        def _(q):
            found = block(wide, q * per_row, (half_rows + r) * per_row, cols)
            for h in range(cols):
                far_pairs[r * cols + h, q] = found[h]

        for h in range(cols):
            mine = me == (half_rows + r) * cols + h

            @pl.when(jnp.logical_not(mine))
            def _():
                cross_copy(r, h).start()

            @pl.when(mine)
            def _():
                cross_local(r, h).start()

    for to_line, to_col in far_order:
        far_copy(to_line, to_col).wait_send()
    for to_line, to_col in near_order:
        main_copy(to_line, to_col).wait_send()
        near_copy(to_line, to_col).wait_send()
    for k in range(half_rows):
        for h in range(cols):

            @pl.when(spot != k * cols + h)
            def _():
                for kind in range(2):
                    same_copy(kind, 0, k, h).wait_send()

            @pl.when(me != (half_rows + k) * cols + h)
            def _():
                cross_copy(k, h).wait_send()

    for k in range(half_rows):

        @pl.when(line == k)
        def _():
            for n in range(places):

                @pl.when(spot != n)
                def _():
                    for chunk in (n, places + n):
                        remote(
                            near_pairs.at[0, 0, pl.ds(0, k + 1)],
                            got_ref.at[1, chunk, pl.ds(0, k + 1)],
                            same_send.at[0, 0], same_recv.at[chunk], row, col,
                        ).wait_recv()

            for kind in range(2):
                same_local(kind, (side if kind == 0 else other) * places + spot, k, 0).wait()

    @pl.when(side == 1)
    def _():
        for n in range(count):

            @pl.when(me != n)
            def _():
                remote(
                    far_pairs.at[0], got_ref.at[0, n], cross_send.at[0], cross_recv.at[n], row, col
                ).wait_recv()

        cross_local(line, col).wait()


def place_kernel(bands, rows, x_ref, o_ref, taken, placed, in_sem, out_sem):
    row, col = lax.axis_index("row"), lax.axis_index("col")
    half_rows = rows // 2
    side = row // half_rows
    chunks = x_ref.shape[1] // bands
    loads = []
    for b in range(bands):
        here = pl.ds(b * chunks, chunks)
        loads.append(pltpu.make_async_copy(x_ref.at[:, here], taken.at[:, here], in_sem.at[b]))
        loads[-1].start()
    index = lax.broadcasted_iota(jnp.int32, (8, LANES), 0)
    second = row * 4 + lax.rem(index, 4)
    stores = []
    for b in range(bands):
        loads[b].wait()
        for p in range(2):
            for q in range(rows):
                keep = q * 4 + col * 2 + index // 4 <= second
                kind = 1 - side if q < half_rows else 1
                for c in range(chunks):
                    pair = taken[kind, b * chunks + c, q % half_rows].astype(jnp.float32)
                    value = jnp.where(keep, pair[p * 8 : p * 8 + 8], 0.0)
                    for k in range(2):
                        placed[b, p, 0, q * 2 + k, :, c * LANES : (c + 1) * LANES] = value[
                            k * 4 : k * 4 + 4
                        ]
            stores.append(
                pltpu.make_async_copy(placed.at[b, p], o_ref.at[b, p], out_sem.at[b, p])
            )
            stores[-1].start()
    for store in stores:
        store.wait()


def exchange_form(rows, cols, spectra, window_flags):
    bands, windows, parts, chans, bins = spectra.shape
    count = rows * cols
    places = count // 2
    half_rows = rows // 2
    height = chans * parts * windows
    dma = pltpu.SemaphoreType.DMA
    got = pl.pallas_call(
        functools.partial(main_kernel, rows, cols),
        out_shape=jax.ShapeDtypeStruct((2, count, half_rows, 16, LANES), jnp.bfloat16),
        in_specs=[
            pl.BlockSpec(memory_space=pl.ANY),
            pl.BlockSpec(memory_space=pltpu.VMEM),
        ],
        out_specs=pl.BlockSpec(memory_space=pl.ANY),
        scratch_shapes=[
            pltpu.VMEM(spectra.shape, spectra.dtype),
            pltpu.VMEM((parts, bins // LANES, windows * chans, LANES), jnp.float32),
            pltpu.VMEM((bands, places, height, LANES), jnp.bfloat16),
            pltpu.VMEM((count, height, LANES), jnp.bfloat16),
            pltpu.VMEM((places, height, LANES), jnp.bfloat16),
            pltpu.VMEM((count * chans, parts, windows, LANES), jnp.float32),
            pltpu.VMEM((places * chans, parts, windows, LANES), jnp.float32),
            pltpu.VMEM((places, half_rows, 16, LANES), jnp.bfloat16),
            pltpu.VMEM((2, places, half_rows, 16, LANES), jnp.bfloat16),
            pltpu.SemaphoreType.REGULAR((rows,)),
            dma((2,)),
            dma((count,)),
            dma((count,)),
            dma((places,)),
            dma((places,)),
            dma((2,)),
            dma((places,)),
            dma((count,)),
            dma,
            dma((2, places)),
            dma((count,)),
            dma((2,)),
        ],
        compiler_params=pltpu.CompilerParams(collective_id=0, has_side_effects=True),
    )(spectra, jnp.transpose(window_flags))
    shape = (bands, 2, 1, rows * chans, cols * chans, bins)
    return pl.pallas_call(
        functools.partial(place_kernel, bands, rows),
        in_specs=[pl.BlockSpec(memory_space=pl.ANY)],
        out_specs=pl.BlockSpec(memory_space=pl.ANY),
        out_shape=jax.ShapeDtypeStruct(shape, jnp.float32),
        scratch_shapes=[
            pltpu.VMEM(got.shape, got.dtype),
            pltpu.VMEM(shape, jnp.float32),
            pltpu.SemaphoreType.DMA((bands,)),
            pltpu.SemaphoreType.DMA((bands, 2)),
        ],
    )(got)


def solution(mesh):
    rows, cols = mesh.shape["row"], mesh.shape["col"]

    def on_device(spectra, window_flags):
        bands, windows, _, chans, bins = spectra.shape
        fits = (
            bands == 2
            and rows % 4 == 0
            and 2 * bins == rows * cols * LANES
            and bins % (2 * LANES) == 0
            and chans == 2
            and cols == 2
            and windows == 32
        )
        if fits:
            return exchange_form(rows, cols, spectra, window_flags)
        return gather_form(spectra, window_flags)

    in_specs = (P("parts", None, None, ("row", "col"), None), P("parts", ("row", "col")))
    out_specs = P("parts", None, "col", None, "row", None)
    return jax.shard_map(
        on_device, mesh=mesh, in_specs=in_specs, out_specs=out_specs, check_vma=False
    )
```

```python
import functools

import jax
import jax.numpy as jnp
from jax import lax
from jax.experimental import pallas as pl
from jax.experimental.pallas import tpu as pltpu
from jax.sharding import PartitionSpec as P

HALFWIN = 64
LANES = 128
epsilon = 1e-06


def window_mean(magnitude):
    bins = magnitude.shape[-1]
    positions = jnp.arange(bins, dtype=jnp.int32)
    near = (jnp.abs(positions[:, None] - positions[None, :]) <= HALFWIN).astype(jnp.float32)
    total = jnp.einsum("...g,gf->...f", magnitude, near, precision=lax.Precision.HIGHEST)
    counted = (
        jnp.minimum(positions + HALFWIN, bins - 1) - jnp.maximum(positions - HALFWIN, 0) + 1
    ).astype(jnp.float32)
    return total / counted


def whiten(values):
    magnitude = jnp.sqrt(values[:, :, 0] * values[:, :, 0] + values[:, :, 1] * values[:, :, 1])
    smooth = window_mean(magnitude)
    return (values / (smooth[:, :, None] + epsilon)).astype(jnp.bfloat16)


def combine_parts(prods, keep):
    real_part = prods[..., 0, 0, :, :, :] + prods[..., 1, 1, :, :, :]
    imag_part = prods[..., 1, 0, :, :, :] - prods[..., 0, 1, :, :, :]
    return jnp.stack([real_part * keep, imag_part * keep], axis=-4)


def gather_form(spectra, window_flags):
    per_device = spectra.shape[3]
    flag_values = window_flags.astype(jnp.float32)[None, :, None, :, None]
    payload = whiten(spectra.astype(jnp.float32) * flag_values)
    row_index = lax.axis_index("row")
    col_index = lax.axis_index("col")
    col_count = lax.axis_size("col")
    row_count = lax.axis_size("row")
    half_size = row_count * per_device
    cols_here = col_count * per_device
    slot = jnp.arange(half_size, dtype=jnp.int32)
    first = (slot // per_device * col_count + col_index) * per_device + slot % per_device
    second = row_index * cols_here + jnp.arange(cols_here, dtype=jnp.int32)
    keep = (first[:, None] <= second[None, :]).astype(jnp.float32)[:, :, None]
    pieces = []
    for band_index in range(spectra.shape[0]):
        first_rows = lax.all_gather(payload[band_index : band_index + 1], "row", axis=3, tiled=True)
        second_rows = lax.all_gather(
            payload[band_index : band_index + 1], "col", axis=3, tiled=True
        )
        prods = jnp.einsum(
            "wpif,wqjf->pqijf", first_rows[0], second_rows[0], preferred_element_type=jnp.float32
        )
        pieces.append(combine_parts(prods, keep))
    result = jnp.stack(pieces, axis=0)
    return result[:, :, None]


def spread_band(x_ref, flag_ref, rows_ref, b):
    _, windows, parts, chans, _ = x_ref.shape
    for w in range(windows):
        for p in range(parts):
            pair = x_ref[b, w, p].astype(jnp.float32)
            for n in range(rows_ref.shape[1]):
                rows_ref[p, n, pl.ds(w * chans, chans)] = pair[:, n * LANES : (n + 1) * LANES]
    extent = (windows, windows)
    same = lax.broadcasted_iota(jnp.int32, extent, 0) == lax.broadcasted_iota(jnp.int32, extent, 1)
    flags = flag_ref[...].astype(jnp.float32)
    return [
        jnp.sum(jnp.where(same, flags[c : c + 1], 0.0), axis=1, keepdims=True)
        for c in range(chans)
    ]


def whiten_band(x_ref, flag_ref, rows_ref, y_ref, b):
    _, windows, _, chans, bins = x_ref.shape
    flags = spread_band(x_ref, flag_ref, rows_ref, b)
    step = 2 * LANES
    chunks = bins // LANES
    near = lax.broadcasted_iota(jnp.int32, (2 * step, step), 0) - LANES
    here = lax.broadcasted_iota(jnp.int32, (2 * step, step), 1)
    inside = (jnp.abs(near - here) <= HALFWIN).astype(jnp.float32).astype(jnp.bfloat16)
    mags = []
    for c in range(chans):
        picked = pl.ds(c, windows, stride=chans)
        line = []
        for n in range(chunks):
            re = rows_ref[0, n, picked] * flags[c]
            im = rows_ref[1, n, picked] * flags[c]
            line.append(jnp.sqrt(re * re + im * im))
        mags.append(jnp.concatenate(line, axis=1))
    mag = jnp.concatenate(mags, axis=0)
    high = mag.astype(jnp.bfloat16)
    low = (mag - high.astype(jnp.float32)).astype(jnp.bfloat16)
    for at in range(0, bins, step):
        start, stop = max(at - LANES, 0), min(at + step + LANES, bins)
        near_rows = inside[start - at + LANES : stop - at + LANES]
        total = jnp.dot(
            high[:, start:stop], near_rows, preferred_element_type=jnp.float32
        ) + jnp.dot(low[:, start:stop], near_rows, preferred_element_type=jnp.float32)
        spot = at + lax.broadcasted_iota(jnp.int32, (1, step), 1)
        counted = (
            jnp.minimum(spot + HALFWIN, bins - 1) - jnp.maximum(spot - HALFWIN, 0) + 1
        ).astype(jnp.float32)
        scale = 1.0 / (total / counted + epsilon)
        for c in range(chans):
            picked = pl.ds(c, windows, stride=chans)
            for p in range(2):
                for half in range(2):
                    lanes = slice(half * LANES, (half + 1) * LANES)
                    value = rows_ref[p, at // LANES + half, picked] * flags[c]
                    out = value * scale[c * windows : (c + 1) * windows, lanes]
                    y_ref[
                        b, at // LANES + half, pl.ds((c * 2 + p) * windows, windows)
                    ] = out.astype(jnp.bfloat16)


def fold(values):
    index = lax.broadcasted_iota(jnp.int32, values[0].shape, 0)
    shift = 1
    while len(values) > 1:
        even = lax.rem(index // shift, 2) == 0
        paired = []
        for n in range(0, len(values), 2):
            u, v = values[n], values[n + 1]
            moved = pltpu.roll(jnp.where(even, v, u), 8 - shift, 0)
            paired.append(jnp.where(even, u, v) + moved)
        values = paired
        shift *= 2
    return values[0]


def by_eight(values):
    total = values[0:8]
    for at in range(8, values.shape[0], 8):
        total = total + values[at : at + 8]
    return total


def block(wide_ref, first, second, cols):
    out = []
    for h in range(cols):
        reals, imags = [], []
        for k in range(2):
            re_a, im_a = wide_ref[first + h * 2 + k, 0], wide_ref[first + h * 2 + k, 1]
            for n in range(cols * 2):
                re_j, im_j = wide_ref[second + n, 0], wide_ref[second + n, 1]
                reals.append(by_eight(re_a * re_j + im_a * im_j))
                imags.append(by_eight(im_a * re_j - re_a * im_j))
        out.append(jnp.concatenate([fold(reals), fold(imags)], axis=0).astype(jnp.bfloat16))
    return out


def main_kernel(
    rows, cols, raw_ref, raw_flags, out_ref, x_ref, flag_ref, spread, sent, held, near_held, wide, got,
    far_pairs, near_pairs, here_sem, in_sem, far_send, far_recv, near_send, near_recv,
    cross_send, cross_recv, cross_own, same_send, same_recv, same_own,
):
    count, half_rows = rows * cols, rows // 2
    places = half_rows * cols
    per_row = cols * 2
    windows = x_ref.shape[1]
    row, col = lax.axis_index("row"), lax.axis_index("col")
    me = row * cols + col
    side, line = row // half_rows, lax.rem(row, half_rows)
    spot = line * cols + col
    other = 1 - side
    upper, lower = side == 1, side == 0

    def remote(src, dst, send_sem, recv_sem, to_row, to_col):
        return pltpu.make_async_remote_copy(
            src_ref=src,
            dst_ref=dst,
            send_sem=send_sem,
            recv_sem=recv_sem,
            device_id={"row": to_row, "col": to_col},
            device_id_type=pl.DeviceIdType.MESH,
        )

    def signal(sem, peer):
        pl.semaphore_signal(
            sem,
            inc=1,
            device_id={"row": peer // cols, "col": lax.rem(peer, cols)},
            device_id_type=pl.DeviceIdType.MESH,
        )

    flag_load = pltpu.make_async_copy(raw_flags, flag_ref, in_sem.at[2])
    flag_load.start()
    loads = []
    for b in range(2):
        loads.append(pltpu.make_async_copy(raw_ref.at[b], x_ref.at[b], in_sem.at[b]))
        loads[b].start()
    barrier = pltpu.get_barrier_semaphore()
    for k in range(1, count):
        peer = lax.rem(me + k, count)

        @pl.when(peer // cols >= row)
        def _():
            signal(barrier, peer)

    pl.semaphore_wait(barrier, row * cols + cols - 1)
    for k in range(1, count):
        peer = lax.rem(me + k, count)

        @pl.when(peer // cols < row)
        def _():
            signal(here_sem.at[row], peer)

    def ready(to_row):
        @pl.when(to_row > row)
        def _():
            pl.semaphore_wait(here_sem.at[to_row], cols)

    def far_copy(to_line, to_col):
        to = to_line * cols + to_col
        return remote(
            sent.at[other, to], held.at[me], far_send.at[other * places + to], far_recv.at[me],
            other * half_rows + to_line, to_col,
        )

    def main_copy(to_line, to_col):
        to = to_line * cols + to_col
        return remote(
            sent.at[side, to], held.at[me], far_send.at[side * places + to], far_recv.at[me],
            side * half_rows + to_line, to_col,
        )

    def near_copy(to_line, to_col):
        to = to_line * cols + to_col
        return remote(
            sent.at[other, to], near_held.at[spot], near_send.at[to], near_recv.at[spot],
            side * half_rows + to_line, to_col,
        )

    far_order = [
        (2 * (i // 2) + lax.rem(row + i, 2), lax.rem(col + j, cols))
        for i in range(half_rows)
        for j in range(cols)
    ]
    near_order = [
        (lax.rem(line + i, half_rows), lax.rem(col + j, cols))
        for i in range(half_rows)
        for j in range(cols)
    ][1:]

    def send_far():
        for n, (to_line, to_col) in enumerate(far_order):
            if n % cols == 0:
                ready(other * half_rows + to_line)
            far_copy(to_line, to_col).start()

    def send_main():
        for n, (to_line, to_col) in enumerate(near_order):
            if n % cols == cols - 1:
                ready(side * half_rows + to_line)
            main_copy(to_line, to_col).start()

    flag_load.wait()
    loads[0].wait()
    whiten_band(x_ref, flag_ref, spread, sent, 0)

    @pl.when(upper)
    def _():
        send_far()

    @pl.when(lower)
    def _():
        send_main()

    loads[1].wait()
    whiten_band(x_ref, flag_ref, spread, sent, 1)

    @pl.when(upper)
    def _():
        send_main()

    @pl.when(lower)
    def _():
        send_far()

    for to_line, to_col in near_order:
        near_copy(to_line, to_col).start()

    def widen(slot, base):
        for c in range(2):
            for p in range(2):
                wide[base + c, p] = slot[pl.ds((c * 2 + p) * windows, windows)].astype(jnp.float32)

    def take(n):
        remote(sent.at[0, 0], held.at[n], far_send.at[0], far_recv.at[n], row, col).wait_recv()
        widen(held.at[n], n * 2)

    def same_copy(kind, k, h):
        to, chunk = k * cols + h, (me if kind == 0 else other * places + spot)
        return remote(
            near_pairs.at[kind, to, pl.ds(0, k + 1)], got.at[1, chunk, pl.ds(0, k + 1)],
            same_send.at[kind, to], same_recv.at[chunk],
            side * half_rows + k, h,
        )

    def same_local(kind, k, h):
        to, chunk = k * cols + h, (me if kind == 0 else other * places + spot)
        return pltpu.make_async_copy(
            near_pairs.at[kind, to, pl.ds(0, k + 1)], got.at[1, chunk, pl.ds(0, k + 1)],
            same_own.at[kind],
        )

    def same(kind, base):
        @pl.loop(0, half_rows)
        def _(step):
            r = lax.rem(line + 1 + step, half_rows)

            @pl.loop(0, r + 1)
            def _(q):
                found = block(wide, base + q * per_row, base + r * per_row, cols)
                for h in range(cols):
                    near_pairs[kind, r * cols + h, q] = found[h]

            for k in range(half_rows):

                @pl.when(r == k)
                def _():
                    for h in range(cols):

                        @pl.when(spot != k * cols + h)
                        def _():
                            same_copy(kind, k, h).start()

                        @pl.when(spot == k * cols + h)
                        def _():
                            same_local(kind, k, h).start()

    def cross_copy(r, h):
        return remote(
            far_pairs.at[r * cols + h], got.at[0, me], cross_send.at[r * cols + h],
            cross_recv.at[me], half_rows + r, h,
        )

    def cross_local(r, h):
        return pltpu.make_async_copy(far_pairs.at[r * cols + h], got.at[0, me], cross_own)

    @pl.when(lower)
    def _():
        for b in range(2):
            for p in range(2):
                out_ref[b, p, 0, half_rows * 2 :] = jnp.zeros(
                    (half_rows * 2,) + out_ref.shape[4:], jnp.float32
                )

    widen(sent.at[side, spot], me * 2)

    @pl.loop(1, places)
    def _(n):
        take(side * places + lax.rem(spot + n, places))

    same(0, side * places * 2)

    widen(sent.at[other, spot], (count + spot) * 2)

    @pl.loop(1, places)
    def _(n):
        at = lax.rem(spot + n, places)
        remote(
            sent.at[0, 0], near_held.at[at], near_send.at[0], near_recv.at[at], row, col
        ).wait_recv()
        widen(near_held.at[at], (count + at) * 2)

    same(1, count * 2)

    @pl.loop(0, half_rows)
    def _(step):
        turn = jnp.where(lower, step // 2, half_rows // 2 - 1 - step // 2)
        line_far = 2 * turn + lax.rem(row + step, 2)
        row_far = other * half_rows + line_far
        for h in range(cols):
            take(row_far * cols + h)

        @pl.loop(0, half_rows)
        def _(j):
            q = side * line_far + other * j
            r = side * j + other * line_far
            found = block(wide, q * per_row, (half_rows + r) * per_row, cols)
            for h in range(cols):
                far_pairs[r * cols + h, q] = found[h]

        @pl.when(lower)
        def _():
            for h in range(cols):
                cross_copy(line_far, h).start()

    @pl.when(upper)
    def _():
        for n, (to_line, to_col) in enumerate(near_order):
            cross_copy(to_line, to_col).start()
        cross_local(line, col).start()

    index = lax.broadcasted_iota(jnp.int32, (8, LANES), 0)
    second = row * per_row + lax.rem(index, per_row)

    def place(kind, chunk, at_row):
        b, lanes = chunk // places, lax.rem(chunk, places) * LANES
        for q in range(half_rows):
            keep = (at_row + q) * per_row + col * 2 + index // per_row <= second
            pair = got[kind, chunk, q].astype(jnp.float32)
            for p in range(2):
                value = jnp.where(keep, pair[p * 8 : p * 8 + 8], 0.0)
                for k in range(2):
                    out_ref[
                        b, p, 0, (at_row + q) * 2 + k, :, pl.ds(pl.multiple_of(lanes, LANES), LANES)
                    ] = value[k * per_row : (k + 1) * per_row]

    def take_same(chunk):
        for k in range(half_rows):

            @pl.when(line == k)
            def _():
                remote(
                    near_pairs.at[0, 0, pl.ds(0, k + 1)], got.at[1, chunk, pl.ds(0, k + 1)],
                    same_send.at[0, 0], same_recv.at[chunk], row, col,
                ).wait_recv()

    def own_same(kind):
        for k in range(half_rows):

            @pl.when(line == k)
            def _():
                same_local(kind, k, 0).wait()

    own_same(0)
    own_same(1)

    @pl.loop(0, count)
    def _(n):
        chunk = lax.rem(me + n, count)

        @pl.when(lax.rem(n, places) > 0)
        def _():
            take_same(chunk)

        place(1, chunk, side * half_rows)

    @pl.when(upper)
    def _():
        cross_local(line, col).wait()
        place(0, me, 0)

        @pl.loop(1, count)
        def _(n):
            chunk = lax.rem(me + n, count)
            remote(
                far_pairs.at[0], got.at[0, chunk], cross_send.at[0], cross_recv.at[chunk], row, col
            ).wait_recv()
            place(0, chunk, 0)

    for to_line, to_col in far_order:
        far_copy(to_line, to_col).wait_send()
    for to_line, to_col in near_order:
        main_copy(to_line, to_col).wait_send()

        near_copy(to_line, to_col).wait_send()
    for k in range(half_rows):
        for h in range(cols):

            @pl.when(spot != k * cols + h)
            def _():
                same_copy(0, k, h).wait_send()
                same_copy(1, k, h).wait_send()

            @pl.when(me != (half_rows + k) * cols + h)
            def _():
                cross_copy(k, h).wait_send()


def exchange_form(rows, cols, spectra, window_flags):
    bands, windows, parts, chans, bins = spectra.shape
    count = rows * cols
    places = count // 2
    half_rows = rows // 2
    height = chans * parts * windows
    dma = pltpu.SemaphoreType.DMA
    shape = (bands, 2, 1, rows * chans, cols * chans, bins)
    return pl.pallas_call(
        functools.partial(main_kernel, rows, cols),
        out_shape=jax.ShapeDtypeStruct(shape, jnp.float32),
        in_specs=[
            pl.BlockSpec(memory_space=pltpu.HBM),
            pl.BlockSpec(memory_space=pltpu.HBM),
        ],
        out_specs=pl.BlockSpec(memory_space=pltpu.VMEM),
        scratch_shapes=[
            pltpu.VMEM(spectra.shape, spectra.dtype),
            pltpu.VMEM((chans, windows), window_flags.dtype),
            pltpu.VMEM((parts, bins // LANES, windows * chans, LANES), jnp.float32),
            pltpu.VMEM((bands, places, height, LANES), jnp.bfloat16),
            pltpu.VMEM((count, height, LANES), jnp.bfloat16),
            pltpu.VMEM((places, height, LANES), jnp.bfloat16),
            pltpu.VMEM(((count + places) * chans, parts, windows, LANES), jnp.float32),
            pltpu.VMEM((2, count, half_rows, 16, LANES), jnp.bfloat16),
            pltpu.VMEM((places, half_rows, 16, LANES), jnp.bfloat16),
            pltpu.VMEM((2, places, half_rows, 16, LANES), jnp.bfloat16),
            pltpu.SemaphoreType.REGULAR((rows,)),
            dma((3,)),
            dma((count,)),
            dma((count,)),
            dma((places,)),
            dma((places,)),
            dma((places,)),
            dma((count,)),
            dma,
            dma((2, places)),
            dma((count,)),
            dma((2,)),
        ],
        compiler_params=pltpu.CompilerParams(
            collective_id=0, has_side_effects=True, vmem_limit_bytes=24 * 1024 * 1024
        ),
    )(
        pltpu.with_memory_space_constraint(spectra, pltpu.HBM),
        pltpu.with_memory_space_constraint(jnp.transpose(window_flags), pltpu.HBM),
    )


def solution(mesh):
    rows, cols = mesh.shape["row"], mesh.shape["col"]

    def on_device(spectra, window_flags):
        bands, windows, _, chans, bins = spectra.shape
        fits = (
            bands == 2
            and rows % 4 == 0
            and 2 * bins == rows * cols * LANES
            and bins % (2 * LANES) == 0
            and chans == 2
            and cols == 2
            and windows == 32
        )
        if fits:
            return exchange_form(rows, cols, spectra, window_flags)
        return gather_form(spectra, window_flags)

    in_specs = (P("parts", None, None, ("row", "col"), None), P("parts", ("row", "col")))
    out_specs = P("parts", None, "col", None, "row", None)
    return jax.shard_map(
        on_device, mesh=mesh, in_specs=in_specs, out_specs=out_specs, check_vma=False
    )
```

```python
import functools

import jax
import jax.numpy as jnp
from jax import lax
from jax.experimental import pallas as pl
from jax.experimental.pallas import tpu as pltpu
from jax.sharding import PartitionSpec as P

HALFWIN = 64
LANES = 128
epsilon = 1e-06


def window_mean(magnitude):
    bins = magnitude.shape[-1]
    positions = jnp.arange(bins, dtype=jnp.int32)
    near = (jnp.abs(positions[:, None] - positions[None, :]) <= HALFWIN).astype(jnp.float32)
    total = jnp.einsum("...g,gf->...f", magnitude, near, precision=lax.Precision.HIGHEST)
    counted = (
        jnp.minimum(positions + HALFWIN, bins - 1) - jnp.maximum(positions - HALFWIN, 0) + 1
    ).astype(jnp.float32)
    return total / counted


def whiten(values):
    magnitude = jnp.sqrt(values[:, :, 0] * values[:, :, 0] + values[:, :, 1] * values[:, :, 1])
    smooth = window_mean(magnitude)
    return (values / (smooth[:, :, None] + epsilon)).astype(jnp.bfloat16)


def combine_parts(prods, keep):
    real_part = prods[..., 0, 0, :, :, :] + prods[..., 1, 1, :, :, :]
    imag_part = prods[..., 1, 0, :, :, :] - prods[..., 0, 1, :, :, :]
    return jnp.stack([real_part * keep, imag_part * keep], axis=-4)


def gather_form(spectra, window_flags):
    per_device = spectra.shape[3]
    flag_values = window_flags.astype(jnp.float32)[None, :, None, :, None]
    payload = whiten(spectra.astype(jnp.float32) * flag_values)
    row_index = lax.axis_index("row")
    col_index = lax.axis_index("col")
    col_count = lax.axis_size("col")
    row_count = lax.axis_size("row")
    half_size = row_count * per_device
    cols_here = col_count * per_device
    slot = jnp.arange(half_size, dtype=jnp.int32)
    first = (slot // per_device * col_count + col_index) * per_device + slot % per_device
    second = row_index * cols_here + jnp.arange(cols_here, dtype=jnp.int32)
    keep = (first[:, None] <= second[None, :]).astype(jnp.float32)[:, :, None]
    pieces = []
    for band_index in range(spectra.shape[0]):
        first_rows = lax.all_gather(payload[band_index : band_index + 1], "row", axis=3, tiled=True)
        second_rows = lax.all_gather(
            payload[band_index : band_index + 1], "col", axis=3, tiled=True
        )
        prods = jnp.einsum(
            "wpif,wqjf->pqijf", first_rows[0], second_rows[0], preferred_element_type=jnp.float32
        )
        pieces.append(combine_parts(prods, keep))
    result = jnp.stack(pieces, axis=0)
    return result[:, :, None]


def spread_band(x_ref, flag_ref, rows_ref, b):
    _, windows, parts, chans, _ = x_ref.shape
    for w in range(windows):
        for p in range(parts):
            pair = x_ref[b, w, p].astype(jnp.float32)
            for n in range(rows_ref.shape[1]):
                rows_ref[p, n, pl.ds(w * chans, chans)] = pair[:, n * LANES : (n + 1) * LANES]
    extent = (windows, windows)
    same = lax.broadcasted_iota(jnp.int32, extent, 0) == lax.broadcasted_iota(jnp.int32, extent, 1)
    flags = flag_ref[...].astype(jnp.float32)
    return [
        jnp.sum(jnp.where(same, flags[c : c + 1], 0.0), axis=1, keepdims=True)
        for c in range(chans)
    ]


def whiten_band(x_ref, flag_ref, rows_ref, y_ref, b):
    _, windows, _, chans, bins = x_ref.shape
    flags = spread_band(x_ref, flag_ref, rows_ref, b)
    step = 2 * LANES
    chunks, group = bins // LANES, y_ref.shape[1]
    near = lax.broadcasted_iota(jnp.int32, (2 * step, step), 0) - LANES
    here = lax.broadcasted_iota(jnp.int32, (2 * step, step), 1)
    inside = (jnp.abs(near - here) <= HALFWIN).astype(jnp.float32).astype(jnp.bfloat16)
    mags = []
    for c in range(chans):
        picked = pl.ds(c, windows, stride=chans)
        line = []
        for n in range(chunks):
            re = rows_ref[0, n, picked] * flags[c]
            im = rows_ref[1, n, picked] * flags[c]
            line.append(jnp.sqrt(re * re + im * im))
        mags.append(jnp.concatenate(line, axis=1))
    mag = jnp.concatenate(mags, axis=0)
    high = mag.astype(jnp.bfloat16)
    low = (mag - high.astype(jnp.float32)).astype(jnp.bfloat16)
    for at in range(0, bins, step):
        start, stop = max(at - LANES, 0), min(at + step + LANES, bins)
        near_rows = inside[start - at + LANES : stop - at + LANES]
        total = jnp.dot(
            high[:, start:stop], near_rows, preferred_element_type=jnp.float32
        ) + jnp.dot(low[:, start:stop], near_rows, preferred_element_type=jnp.float32)
        spot = at + lax.broadcasted_iota(jnp.int32, (1, step), 1)
        counted = (
            jnp.minimum(spot + HALFWIN, bins - 1) - jnp.maximum(spot - HALFWIN, 0) + 1
        ).astype(jnp.float32)
        scale = 1.0 / (total / counted + epsilon)
        for c in range(chans):
            picked = pl.ds(c, windows, stride=chans)
            for p in range(2):
                for half in range(2):
                    lanes = slice(half * LANES, (half + 1) * LANES)
                    value = rows_ref[p, at // LANES + half, picked] * flags[c]
                    out = value * scale[c * windows : (c + 1) * windows, lanes]
                    chunk = at // LANES + half
                    y_ref[
                        b, chunk % group, chunk // group, pl.ds((c * 2 + p) * windows, windows)
                    ] = out.astype(jnp.bfloat16)


def fold(values):
    index = lax.broadcasted_iota(jnp.int32, values[0].shape, 0)
    shift = 1
    while len(values) > 1:
        even = lax.rem(index // shift, 2) == 0
        paired = []
        for n in range(0, len(values), 2):
            u, v = values[n], values[n + 1]
            moved = pltpu.roll(jnp.where(even, v, u), 8 - shift, 0)
            paired.append(jnp.where(even, u, v) + moved)
        values = paired
        shift *= 2
    return values[0]


def by_eight(values):
    total = values[0:8]
    for at in range(8, values.shape[0], 8):
        total = total + values[at : at + 8]
    return total


def block(wide_ref, first, second, cols):
    out = []
    for h in range(cols):
        reals, imags = [], []
        for k in range(2):
            re_a, im_a = wide_ref[first + h * 2 + k, 0], wide_ref[first + h * 2 + k, 1]
            for n in range(cols * 2):
                re_j, im_j = wide_ref[second + n, 0], wide_ref[second + n, 1]
                reals.append(by_eight(re_a * re_j + im_a * im_j))
                imags.append(by_eight(im_a * re_j - re_a * im_j))
        out.append(jnp.concatenate([fold(reals), fold(imags)], axis=0).astype(jnp.bfloat16))
    return out


def main_kernel(
    rows, cols, raw_ref, raw_flags, out_ref, x_ref, flag_ref, spread, sent, held, near_held, wide,
    got, far_pairs, near_pairs, here_sem, in_sem, far_send, main_send, far_recv, pass_send,
    near_send, near_recv, cross_send, cross_recv, cross_own, same_send, same_recv, same_own,
):
    count, half_rows, plane_rows = rows * cols, rows // 2, rows // 4
    places, group = half_rows * cols, plane_rows * cols
    per_row = cols * 2
    windows = x_ref.shape[1]
    row, col = lax.axis_index("row"), lax.axis_index("col")
    me = row * cols + col
    side, line = row // half_rows, lax.rem(row, half_rows)
    spot = line * cols + col
    other = 1 - side
    plane, seat = line // plane_rows, lax.rem(spot, group)
    inner, outer = plane == other, plane == side
    upper, lower = side == 1, side == 0

    def remote(src, dst, send_sem, recv_sem, to_row, to_col):
        return pltpu.make_async_remote_copy(
            src_ref=src,
            dst_ref=dst,
            send_sem=send_sem,
            recv_sem=recv_sem,
            device_id={"row": to_row, "col": to_col},
            device_id_type=pl.DeviceIdType.MESH,
        )

    def signal(sem, peer):
        pl.semaphore_signal(
            sem,
            inc=1,
            device_id={"row": peer // cols, "col": lax.rem(peer, cols)},
            device_id_type=pl.DeviceIdType.MESH,
        )

    flag_load = pltpu.make_async_copy(raw_flags, flag_ref, in_sem.at[2])
    flag_load.start()
    loads = []
    for n, b in enumerate((other, side)):
        loads.append(pltpu.make_async_copy(raw_ref.at[b], x_ref.at[b], in_sem.at[n]))
        loads[n].start()
    barrier = pltpu.get_barrier_semaphore()
    for k in range(1, count):
        peer = lax.rem(me + k, count)

        @pl.when(peer // cols >= row)
        def _():
            signal(barrier, peer)

    pl.semaphore_wait(barrier, row * cols + cols - 1)
    for k in range(1, count):
        peer = lax.rem(me + k, count)

        @pl.when(peer // cols < row)
        def _():
            signal(here_sem.at[row], peer)

    def ready(to_row):
        @pl.when(to_row > row)
        def _():
            pl.semaphore_wait(here_sem.at[to_row], cols)

    def far_copy(to_plane, to_seat):
        to = to_plane * group + to_seat
        return remote(
            sent.at[other, to_seat, to_plane], held.at[me], far_send.at[to], far_recv.at[me],
            other * half_rows + to // cols, lax.rem(to_seat, cols),
        )

    def pass_copy(from_seat, to_plane):
        source = side * group + from_seat
        return remote(
            near_held.at[source, to_plane], held.at[side * places + source],
            pass_send.at[from_seat * 2 + to_plane], far_recv.at[side * places + source],
            other * half_rows + to_plane * plane_rows + seat // cols, col,
        )

    def near_copy(to_seat):
        return remote(
            sent.at[other, to_seat], near_held.at[spot], near_send.at[to_seat], near_recv.at[spot],
            side * half_rows + other * plane_rows + to_seat // cols, lax.rem(to_seat, cols),
        )

    def main_copy(to_line, to_col):
        to = to_line * cols + to_col
        return remote(
            sent.at[side, lax.rem(to, group), to // group], held.at[me], main_send.at[to],
            far_recv.at[me], side * half_rows + to_line, to_col,
        )

    seats = [
        lax.rem(line + i, plane_rows) * cols + lax.rem(col + j, cols)
        for i in range(plane_rows)
        for j in range(cols)
    ]
    near_order = [
        (lax.rem(line + i, half_rows), lax.rem(col + j, cols))
        for i in range(half_rows)
        for j in range(cols)
    ][1:]

    def send_far(to_plane):
        for n, to_seat in enumerate(seats):
            if n % cols == 0:
                ready(other * half_rows + to_plane * plane_rows + to_seat // cols)
            far_copy(to_plane, to_seat).start()

    flag_load.wait()
    loads[0].wait()
    whiten_band(x_ref, flag_ref, spread, sent, other)

    @pl.when(inner)
    def _():
        send_far(side)

    @pl.when(outer)
    def _():
        for n, to_seat in enumerate(seats):
            if n % cols == 0:
                ready(side * half_rows + other * plane_rows + to_seat // cols)
            near_copy(to_seat).start()

    loads[1].wait()
    whiten_band(x_ref, flag_ref, spread, sent, side)
    for n, (to_line, to_col) in enumerate(near_order):
        if n % cols == cols - 1:

            @pl.when(inner | (to_line // plane_rows == plane))
            def _():
                ready(side * half_rows + to_line)

        main_copy(to_line, to_col).start()

    @pl.when(inner)
    def _():
        send_far(other)
        for to_seat in seats[1:]:
            near_copy(to_seat).start()

    def widen(slot, base):
        for c in range(2):
            for p in range(2):
                wide[base + c, p] = slot[pl.ds((c * 2 + p) * windows, windows)].astype(jnp.float32)

    def take(n):
        remote(
            sent.at[0, 0, 0], held.at[n], far_send.at[0], far_recv.at[n], row, col
        ).wait_recv()
        widen(held.at[n], n * 2)

    def take_near(source):
        remote(
            sent.at[0, 0], near_held.at[source], near_send.at[0], near_recv.at[source], row, col
        ).wait_recv()

    def widen_near(source, ref):
        for z in range(2):
            widen(ref.at[z], (count + z * places + source) * 2)

    @pl.when(inner)
    def _():
        @pl.loop(0, group)
        def _(n):
            from_seat = lax.rem(seat + n, group)
            source = side * group + from_seat
            take_near(source)
            for z in range(2):
                pass_copy(from_seat, z).start()
            widen_near(source, near_held.at[source])

    def chunk_of(kind):
        return me if kind == 0 else other * places + (kind - 1) * group + seat

    def same_copy(kind, k, h):
        to, chunk = k * cols + h, chunk_of(kind)
        return remote(
            near_pairs.at[kind, to, pl.ds(0, k + 1)], got.at[1, chunk, pl.ds(0, k + 1)],
            same_send.at[kind, to], same_recv.at[chunk], side * half_rows + k, h,
        )

    def same_local(kind, k, h):
        to, chunk = k * cols + h, chunk_of(kind)
        return pltpu.make_async_copy(
            near_pairs.at[kind, to, pl.ds(0, k + 1)], got.at[1, chunk, pl.ds(0, k + 1)],
            same_own.at[kind],
        )

    def same(kind, base):
        @pl.loop(0, half_rows)
        def _(step):
            r = lax.rem(line + 1 + step, half_rows)

            @pl.loop(0, r + 1)
            def _(q):
                found = block(wide, base + q * per_row, base + r * per_row, cols)
                for h in range(cols):
                    near_pairs[kind, r * cols + h, q] = found[h]

            for k in range(half_rows):

                @pl.when(r == k)
                def _():
                    for h in range(cols):

                        @pl.when(spot != k * cols + h)
                        def _():
                            same_copy(kind, k, h).start()

                        @pl.when(spot == k * cols + h)
                        def _():
                            same_local(kind, k, h).start()

    def cross_copy(r, h):
        return remote(
            far_pairs.at[r * cols + h], got.at[0, me], cross_send.at[r * cols + h],
            cross_recv.at[me], half_rows + r, h,
        )

    def cross_local(r, h):
        return pltpu.make_async_copy(far_pairs.at[r * cols + h], got.at[0, me], cross_own)

    @pl.when(lower)
    def _():
        for b in range(2):
            for p in range(2):
                out_ref[b, p, 0, half_rows * 2 :] = jnp.zeros(
                    (half_rows * 2,) + out_ref.shape[4:], jnp.float32
                )

    widen(sent.at[side, seat, plane], me * 2)

    @pl.loop(1, places)
    def _(n):
        take(side * places + lax.rem(spot + n, places))

    same(0, side * places * 2)

    @pl.when(inner)
    def _():
        widen_near(spot, sent.at[other, seat])

        @pl.loop(1, group)
        def _(n):
            source = other * group + lax.rem(seat + n, group)
            take_near(source)
            widen_near(source, near_held.at[source])

        for z in range(2):
            same(1 + z, (count + z * places) * 2)

    @pl.when(outer)
    def _():
        for n in range(half_rows):
            ready(other * half_rows + n)

    @pl.loop(0, half_rows)
    def _(step):
        turn = jnp.where(lower, step // 2, half_rows // 2 - 1 - step // 2)
        line_far = 2 * turn + lax.rem(row + step, 2)
        row_far = other * half_rows + line_far
        for h in range(cols):
            take(row_far * cols + h)

        @pl.loop(0, half_rows)
        def _(j):
            q = side * line_far + other * j
            r = side * j + other * line_far
            found = block(wide, q * per_row, (half_rows + r) * per_row, cols)
            for h in range(cols):
                far_pairs[r * cols + h, q] = found[h]

        @pl.when(lower)
        def _():
            for h in range(cols):
                cross_copy(line_far, h).start()

    @pl.when(upper)
    def _():
        for n, (to_line, to_col) in enumerate(near_order):
            cross_copy(to_line, to_col).start()
        cross_local(line, col).start()

    index = lax.broadcasted_iota(jnp.int32, (8, LANES), 0)
    second = row * per_row + lax.rem(index, per_row)

    def place(kind, chunk, at_row):
        b, lanes = chunk // places, lax.rem(chunk, places) * LANES
        for q in range(half_rows):
            keep = (at_row + q) * per_row + col * 2 + index // per_row <= second
            pair = got[kind, chunk, q].astype(jnp.float32)
            for p in range(2):
                value = jnp.where(keep, pair[p * 8 : p * 8 + 8], 0.0)
                for k in range(2):
                    out_ref[
                        b, p, 0, (at_row + q) * 2 + k, :, pl.ds(pl.multiple_of(lanes, LANES), LANES)
                    ] = value[k * per_row : (k + 1) * per_row]

    def take_same(chunk):
        for k in range(half_rows):

            @pl.when(line == k)
            def _():
                remote(
                    near_pairs.at[0, 0, pl.ds(0, k + 1)], got.at[1, chunk, pl.ds(0, k + 1)],
                    same_send.at[0, 0], same_recv.at[chunk], row, col,
                ).wait_recv()

    def own_same(kind):
        for k in range(half_rows):

            @pl.when(line == k)
            def _():
                same_local(kind, k, 0).wait()

    own_same(0)

    @pl.when(inner)
    def _():
        own_same(1)
        own_same(2)

    @pl.loop(0, count)
    def _(n):
        chunk = lax.rem(me + n, count)
        ours = lax.rem(n, group) == 0

        @pl.when(jnp.logical_not((n == 0) | (inner & ours & (chunk // places == other))))
        def _():
            take_same(chunk)

        place(1, chunk, side * half_rows)

    @pl.when(upper)
    def _():
        cross_local(line, col).wait()
        place(0, me, 0)

        @pl.loop(1, count)
        def _(n):
            chunk = lax.rem(me + n, count)
            remote(
                far_pairs.at[0], got.at[0, chunk], cross_send.at[0], cross_recv.at[chunk], row, col
            ).wait_recv()
            place(0, chunk, 0)

    for to_line, to_col in near_order:
        main_copy(to_line, to_col).wait_send()
    for to_seat in seats[1:]:
        near_copy(to_seat).wait_send()

    @pl.when(outer)
    def _():
        near_copy(seats[0]).wait_send()

    @pl.when(inner)
    def _():
        for to_seat in seats:
            for z in range(2):
                far_copy(z, to_seat).wait_send()
                pass_copy(to_seat, z).wait_send()

    for k in range(half_rows):
        for h in range(cols):

            @pl.when(spot != k * cols + h)
            def _():
                same_copy(0, k, h).wait_send()

                @pl.when(inner)
                def _():
                    same_copy(1, k, h).wait_send()
                    same_copy(2, k, h).wait_send()

            @pl.when(me != (half_rows + k) * cols + h)
            def _():
                cross_copy(k, h).wait_send()


def exchange_form(rows, cols, spectra, window_flags):
    bands, windows, parts, chans, bins = spectra.shape
    count = rows * cols
    places = count // 2
    half_rows, group = rows // 2, places // 2
    height = chans * parts * windows
    dma = pltpu.SemaphoreType.DMA
    shape = (bands, 2, 1, rows * chans, cols * chans, bins)
    return pl.pallas_call(
        functools.partial(main_kernel, rows, cols),
        out_shape=jax.ShapeDtypeStruct(shape, jnp.float32),
        in_specs=[
            pl.BlockSpec(memory_space=pltpu.HBM),
            pl.BlockSpec(memory_space=pltpu.HBM),
        ],
        out_specs=pl.BlockSpec(memory_space=pltpu.VMEM),
        scratch_shapes=[
            pltpu.VMEM(spectra.shape, spectra.dtype),
            pltpu.VMEM((chans, windows), window_flags.dtype),
            pltpu.VMEM((parts, bins // LANES, windows * chans, LANES), jnp.float32),
            pltpu.VMEM((bands, group, 2, height, LANES), jnp.bfloat16),
            pltpu.VMEM((count, height, LANES), jnp.bfloat16),
            pltpu.VMEM((places, 2, height, LANES), jnp.bfloat16),
            pltpu.VMEM(((count + places * 2) * chans, parts, windows, LANES), jnp.float32),
            pltpu.VMEM((2, count, half_rows, 16, LANES), jnp.bfloat16),
            pltpu.VMEM((places, half_rows, 16, LANES), jnp.bfloat16),
            pltpu.VMEM((3, places, half_rows, 16, LANES), jnp.bfloat16),
            pltpu.SemaphoreType.REGULAR((rows,)),
            dma((3,)),
            dma((places,)),
            dma((places,)),
            dma((count,)),
            dma((places,)),
            dma((group,)),
            dma((places,)),
            dma((places,)),
            dma((count,)),
            dma,
            dma((3, places)),
            dma((count,)),
            dma((3,)),
        ],
        compiler_params=pltpu.CompilerParams(
            collective_id=0, has_side_effects=True, vmem_limit_bytes=24 * 1024 * 1024
        ),
    )(
        pltpu.with_memory_space_constraint(spectra, pltpu.HBM),
        pltpu.with_memory_space_constraint(jnp.transpose(window_flags), pltpu.HBM),
    )


def solution(mesh):
    rows, cols = mesh.shape["row"], mesh.shape["col"]

    def on_device(spectra, window_flags):
        bands, windows, _, chans, bins = spectra.shape
        fits = (
            bands == 2
            and rows % 4 == 0
            and 2 * bins == rows * cols * LANES
            and bins % (2 * LANES) == 0
            and chans == 2
            and cols == 2
            and windows == 32
        )
        if fits:
            return exchange_form(rows, cols, spectra, window_flags)
        return gather_form(spectra, window_flags)

    in_specs = (P("parts", None, None, ("row", "col"), None), P("parts", ("row", "col")))
    out_specs = P("parts", None, "col", None, "row", None)
    return jax.shard_map(
        on_device, mesh=mesh, in_specs=in_specs, out_specs=out_specs, check_vma=False
    )
```

```python
import functools

import jax
import jax.numpy as jnp
from jax import lax
from jax.experimental import pallas as pl
from jax.experimental.pallas import tpu as pltpu
from jax.sharding import PartitionSpec as P

HALFWIN = 64
LANES = 128
epsilon = 1e-06


def window_mean(magnitude):
    bins = magnitude.shape[-1]
    positions = jnp.arange(bins, dtype=jnp.int32)
    near = (jnp.abs(positions[:, None] - positions[None, :]) <= HALFWIN).astype(jnp.float32)
    total = jnp.einsum("...g,gf->...f", magnitude, near, precision=lax.Precision.HIGHEST)
    counted = (
        jnp.minimum(positions + HALFWIN, bins - 1) - jnp.maximum(positions - HALFWIN, 0) + 1
    ).astype(jnp.float32)
    return total / counted


def whiten(values):
    magnitude = jnp.sqrt(values[:, :, 0] * values[:, :, 0] + values[:, :, 1] * values[:, :, 1])
    smooth = window_mean(magnitude)
    return (values / (smooth[:, :, None] + epsilon)).astype(jnp.bfloat16)


def combine_parts(prods, keep):
    real_part = prods[..., 0, 0, :, :, :] + prods[..., 1, 1, :, :, :]
    imag_part = prods[..., 1, 0, :, :, :] - prods[..., 0, 1, :, :, :]
    return jnp.stack([real_part * keep, imag_part * keep], axis=-4)


def gather_form(spectra, window_flags):
    per_device = spectra.shape[3]
    flag_values = window_flags.astype(jnp.float32)[None, :, None, :, None]
    payload = whiten(spectra.astype(jnp.float32) * flag_values)
    row_index = lax.axis_index("row")
    col_index = lax.axis_index("col")
    col_count = lax.axis_size("col")
    row_count = lax.axis_size("row")
    half_size = row_count * per_device
    cols_here = col_count * per_device
    slot = jnp.arange(half_size, dtype=jnp.int32)
    first = (slot // per_device * col_count + col_index) * per_device + slot % per_device
    second = row_index * cols_here + jnp.arange(cols_here, dtype=jnp.int32)
    keep = (first[:, None] <= second[None, :]).astype(jnp.float32)[:, :, None]
    pieces = []
    for band_index in range(spectra.shape[0]):
        first_rows = lax.all_gather(payload[band_index : band_index + 1], "row", axis=3, tiled=True)
        second_rows = lax.all_gather(
            payload[band_index : band_index + 1], "col", axis=3, tiled=True
        )
        prods = jnp.einsum(
            "wpif,wqjf->pqijf", first_rows[0], second_rows[0], preferred_element_type=jnp.float32
        )
        pieces.append(combine_parts(prods, keep))
    result = jnp.stack(pieces, axis=0)
    return result[:, :, None]


def spread_band(x_ref, flag_ref, rows_ref, b):
    _, windows, parts, chans, _ = x_ref.shape
    for w in range(windows):
        for p in range(parts):
            pair = x_ref[b, w, p].astype(jnp.float32)
            for n in range(rows_ref.shape[1]):
                rows_ref[p, n, pl.ds(w * chans, chans)] = pair[:, n * LANES : (n + 1) * LANES]
    extent = (windows, windows)
    same = lax.broadcasted_iota(jnp.int32, extent, 0) == lax.broadcasted_iota(jnp.int32, extent, 1)
    flags = flag_ref[...].astype(jnp.float32)
    return [
        jnp.sum(jnp.where(same, flags[c : c + 1], 0.0), axis=1, keepdims=True)
        for c in range(chans)
    ]


def whiten_band(x_ref, flag_ref, rows_ref, y_ref, b):
    _, windows, _, chans, bins = x_ref.shape
    flags = spread_band(x_ref, flag_ref, rows_ref, b)
    step = 2 * LANES
    chunks, group = bins // LANES, y_ref.shape[1]
    near = lax.broadcasted_iota(jnp.int32, (2 * step, step), 0) - LANES
    here = lax.broadcasted_iota(jnp.int32, (2 * step, step), 1)
    inside = (jnp.abs(near - here) <= HALFWIN).astype(jnp.float32).astype(jnp.bfloat16)
    mags = []
    for c in range(chans):
        picked = pl.ds(c, windows, stride=chans)
        line = []
        for n in range(chunks):
            re = rows_ref[0, n, picked] * flags[c]
            im = rows_ref[1, n, picked] * flags[c]
            line.append(jnp.sqrt(re * re + im * im))
        mags.append(jnp.concatenate(line, axis=1))
    mag = jnp.concatenate(mags, axis=0)
    high = mag.astype(jnp.bfloat16)
    low = (mag - high.astype(jnp.float32)).astype(jnp.bfloat16)
    for at in range(0, bins, step):
        start, stop = max(at - LANES, 0), min(at + step + LANES, bins)
        near_rows = inside[start - at + LANES : stop - at + LANES]
        total = jnp.dot(
            high[:, start:stop], near_rows, preferred_element_type=jnp.float32
        ) + jnp.dot(low[:, start:stop], near_rows, preferred_element_type=jnp.float32)
        spot = at + lax.broadcasted_iota(jnp.int32, (1, step), 1)
        counted = (
            jnp.minimum(spot + HALFWIN, bins - 1) - jnp.maximum(spot - HALFWIN, 0) + 1
        ).astype(jnp.float32)
        scale = 1.0 / (total / counted + epsilon)
        for c in range(chans):
            picked = pl.ds(c, windows, stride=chans)
            for p in range(2):
                for half in range(2):
                    lanes = slice(half * LANES, (half + 1) * LANES)
                    value = rows_ref[p, at // LANES + half, picked] * flags[c]
                    out = value * scale[c * windows : (c + 1) * windows, lanes]
                    chunk = at // LANES + half
                    y_ref[
                        b, chunk % group, chunk // group, pl.ds((c * 2 + p) * windows, windows)
                    ] = out.astype(jnp.bfloat16)


def fold(values):
    index = lax.broadcasted_iota(jnp.int32, values[0].shape, 0)
    shift = 1
    while len(values) > 1:
        even = lax.rem(index // shift, 2) == 0
        paired = []
        for n in range(0, len(values), 2):
            u, v = values[n], values[n + 1]
            moved = pltpu.roll(jnp.where(even, v, u), 8 - shift, 0)
            paired.append(jnp.where(even, u, v) + moved)
        values = paired
        shift *= 2
    return values[0]


def by_eight(values):
    total = values[0:8]
    for at in range(8, values.shape[0], 8):
        total = total + values[at : at + 8]
    return total


def block(wide_ref, first, second, cols):
    out = []
    for h in range(cols):
        reals, imags = [], []
        for k in range(2):
            re_a, im_a = wide_ref[first + h * 2 + k, 0], wide_ref[first + h * 2 + k, 1]
            for n in range(cols * 2):
                re_j, im_j = wide_ref[second + n, 0], wide_ref[second + n, 1]
                reals.append(by_eight(re_a * re_j + im_a * im_j))
                imags.append(by_eight(im_a * re_j - re_a * im_j))
        out.append(jnp.concatenate([fold(reals), fold(imags)], axis=0).astype(jnp.bfloat16))
    return out


def main_kernel(
    rows, cols, raw_ref, raw_flags, out_ref, x_ref, flag_ref, spread, sent, held, near_held, wide,
    got, far_pairs, near_pairs, here_sem, go_sem, in_sem, main_send, far_recv, pass_send,
    near_send, near_recv, cross_send, cross_recv, cross_own, same_send, same_recv, same_own,
):
    count, half_rows, plane_rows = rows * cols, rows // 2, rows // 4
    places, group = half_rows * cols, plane_rows * cols
    per_row = cols * 2
    windows = x_ref.shape[1]
    row, col = lax.axis_index("row"), lax.axis_index("col")
    me = row * cols + col
    side, line = row // half_rows, lax.rem(row, half_rows)
    spot = line * cols + col
    other = 1 - side
    plane, seat = line // plane_rows, lax.rem(spot, group)
    inner, outer = plane == other, plane == side
    upper, lower = side == 1, side == 0

    def remote(src, dst, send_sem, recv_sem, to_row, to_col):
        return pltpu.make_async_remote_copy(
            src_ref=src,
            dst_ref=dst,
            send_sem=send_sem,
            recv_sem=recv_sem,
            device_id={"row": to_row, "col": to_col},
            device_id_type=pl.DeviceIdType.MESH,
        )

    def signal(sem, peer):
        pl.semaphore_signal(
            sem,
            inc=1,
            device_id={"row": peer // cols, "col": lax.rem(peer, cols)},
            device_id_type=pl.DeviceIdType.MESH,
        )

    flag_load = pltpu.make_async_copy(raw_flags, flag_ref, in_sem.at[2])
    flag_load.start()
    loads = []
    for n, b in enumerate((other, side)):
        loads.append(pltpu.make_async_copy(raw_ref.at[b], x_ref.at[b], in_sem.at[n]))
        loads[n].start()
    def turn_of(peer):
        return peer // cols * cols + cols - 1 - lax.rem(peer, cols)

    barrier = pltpu.get_barrier_semaphore()
    for k in range(1, count):
        peer = lax.rem(me + k, count)

        @pl.when(turn_of(peer) > turn_of(me))
        def _():
            signal(barrier, peer)

    @pl.when(turn_of(me) > 0)
    def _():
        pl.semaphore_wait(barrier, turn_of(me))

    for k in range(count):
        peer = lax.rem(row * cols + cols - 1 + count - k, count)

        @pl.when(turn_of(peer) < turn_of(me))
        def _():
            signal(here_sem.at[me], peer)

    def ready(peer):
        @pl.when(turn_of(peer) > turn_of(me))
        def _():
            pl.semaphore_wait(here_sem.at[peer], 1)

    def pass_copy(source, z, src):
        return remote(
            src, held.at[side * places + source], pass_send.at[source * 2 + z],
            far_recv.at[side * places + source],
            other * half_rows + z * plane_rows + seat // cols, col,
        )

    def near_copy(to_seat, z):
        return remote(
            sent.at[other, to_seat, z], near_held.at[spot, z], near_send.at[to_seat * 2 + z],
            near_recv.at[spot * 2 + z],
            side * half_rows + other * plane_rows + to_seat // cols, lax.rem(to_seat, cols),
        )

    def main_copy(to):
        return remote(
            sent.at[side, lax.rem(to, group), to // group], held.at[me], main_send.at[to],
            far_recv.at[me], side * half_rows + to // cols, lax.rem(to, cols),
        )

    seats = [
        lax.rem(line + i, plane_rows) * cols + lax.rem(col + j, cols)
        for i in range(plane_rows)
        for j in range(cols)
    ]
    near_order = [
        (to_plane * group + to_seat) for to_plane in (plane, 1 - plane) for to_seat in seats
    ][1:]

    def send_near(to_seats):
        for to_seat in to_seats:
            ready(side * places + other * group + to_seat)
            for z in range(2):
                near_copy(to_seat, z).start()

    def send_own(z):
        ready(other * places + z * group + seat)
        pass_copy(spot, z, sent.at[other, seat, z]).start()

    flag_load.wait()
    loads[0].wait()
    whiten_band(x_ref, flag_ref, spread, sent, other)

    @pl.when(inner)
    def _():
        send_near(seats[1:])
        send_own(side)

    @pl.when(outer)
    def _():
        send_near(seats)

    loads[1].wait()
    whiten_band(x_ref, flag_ref, spread, sent, side)
    for to in near_order:

        @pl.when(to // group == side)
        def _():
            ready(side * places + to)

        main_copy(to).start()

    @pl.when(inner)
    def _():
        send_own(other)

    def widen(slot, base):
        for c in range(2):
            for p in range(2):
                wide[base + c, p] = slot[pl.ds((c * 2 + p) * windows, windows)].astype(jnp.float32)

    def take(n):
        remote(
            sent.at[0, 0, 0], held.at[n], main_send.at[0], far_recv.at[n], row, col
        ).wait_recv()
        widen(held.at[n], n * 2)

    def take_near(source, z):
        remote(
            sent.at[0, 0, 0], near_held.at[source, z], near_send.at[0],
            near_recv.at[source * 2 + z], row, col,
        ).wait_recv()

    def widen_near(source, ref, z):
        widen(ref.at[z], (count + z * places + source) * 2)

    near_sources = [other * group + n for n in seats[1:]] + [side * group + n for n in seats]

    @pl.when(inner)
    def _():
        for source in near_sources:
            for z in range(2):
                take_near(source, z)
                pass_copy(source, z, near_held.at[source, z]).start()
                widen_near(source, near_held.at[source], z)

    def chunk_of(kind):
        return me if kind == 0 else other * places + (kind - 1) * group + seat

    def same_copy(kind, k, h):
        to, chunk = k * cols + h, chunk_of(kind)
        return remote(
            near_pairs.at[kind, to, pl.ds(0, k + 1)], got.at[1, chunk, pl.ds(0, k + 1)],
            same_send.at[kind, to], same_recv.at[chunk], side * half_rows + k, h,
        )

    def same_local(kind, k, h):
        to, chunk = k * cols + h, chunk_of(kind)
        return pltpu.make_async_copy(
            near_pairs.at[kind, to, pl.ds(0, k + 1)], got.at[1, chunk, pl.ds(0, k + 1)],
            same_own.at[kind],
        )

    def same(kind, base):
        @pl.loop(0, half_rows)
        def _(step):
            r = lax.rem(line + 1 + step, half_rows)

            @pl.loop(0, r + 1)
            def _(q):
                found = block(wide, base + q * per_row, base + r * per_row, cols)
                for h in range(cols):
                    near_pairs[kind, r * cols + h, q] = found[h]

            for k in range(half_rows):

                @pl.when(r == k)
                def _():
                    for h in range(cols):

                        @pl.when(spot != k * cols + h)
                        def _():
                            same_copy(kind, k, h).start()

                        @pl.when(spot == k * cols + h)
                        def _():
                            same_local(kind, k, h).start()

    def cross_copy(r, h):
        return remote(
            far_pairs.at[r * cols + h], got.at[0, me], cross_send.at[r * cols + h],
            cross_recv.at[me], half_rows + r, h,
        )

    def cross_local(r, h):
        return pltpu.make_async_copy(far_pairs.at[r * cols + h], got.at[0, me], cross_own)

    @pl.when(lower)
    def _():
        for b in range(2):
            for p in range(2):
                out_ref[b, p, 0, half_rows * 2 :] = jnp.zeros(
                    (half_rows * 2,) + out_ref.shape[4:], jnp.float32
                )

    @pl.when(inner)
    def _():
        for z in range(2):
            widen_near(spot, sent.at[other, seat], z)
        for z in range(2):
            same(1 + z, (count + z * places) * 2)

    widen(sent.at[side, seat, plane], me * 2)

    @pl.loop(1, places)
    def _(n):
        take(side * places + lax.rem(spot + n, places))

    same(0, side * places * 2)

    for n in range(places):

        @pl.when(outer | (n % group != seat))
        def _():
            ready(other * places + n)

    def pass_sent():
        for source in [spot] + near_sources:
            for z in range(2):
                pass_copy(source, z, near_held.at[0, 0]).wait_send()

    @pl.loop(0, half_rows)
    def _(step):
        turn = jnp.where(lower, step // 2, half_rows // 2 - 1 - step // 2)
        line_far = 2 * turn + lax.rem(row + step, 2)
        row_far = other * half_rows + line_far
        for h in range(cols):
            take(row_far * cols + h)

        @pl.loop(0, half_rows)
        def _(j):
            q = side * line_far + other * j
            r = side * j + other * line_far
            found = block(wide, q * per_row, (half_rows + r) * per_row, cols)
            for h in range(cols):
                far_pairs[r * cols + h, q] = found[h]

        @pl.when(lower & inner & (step == 0))
        def _():
            pass_sent()
            signal(go_sem, side * places + side * group + seat)

        @pl.when(lower & outer & (step == 0))
        def _():
            pl.semaphore_wait(go_sem, 1)

        @pl.when(lower)
        def _():
            for h in range(cols):
                cross_copy(line_far, h).start()

    @pl.when(upper)
    def _():
        for to in near_order[::-1]:
            cross_copy(to // cols, lax.rem(to, cols)).start()
        cross_local(line, col).start()

    index = lax.broadcasted_iota(jnp.int32, (8, LANES), 0)
    second = row * per_row + lax.rem(index, per_row)

    def place(kind, chunk, at_row):
        b, lanes = chunk // places, lax.rem(chunk, places) * LANES
        for q in range(half_rows):
            keep = (at_row + q) * per_row + col * 2 + index // per_row <= second
            pair = got[kind, chunk, q].astype(jnp.float32)
            for p in range(2):
                value = jnp.where(keep, pair[p * 8 : p * 8 + 8], 0.0)
                for k in range(2):
                    out_ref[
                        b, p, 0, (at_row + q) * 2 + k, :, pl.ds(pl.multiple_of(lanes, LANES), LANES)
                    ] = value[k * per_row : (k + 1) * per_row]

    def take_same(chunk):
        for k in range(half_rows):

            @pl.when(line == k)
            def _():
                remote(
                    near_pairs.at[0, 0, pl.ds(0, k + 1)], got.at[1, chunk, pl.ds(0, k + 1)],
                    same_send.at[0, 0], same_recv.at[chunk], row, col,
                ).wait_recv()

    def own_same(kind):
        for k in range(half_rows):

            @pl.when(line == k)
            def _():
                same_local(kind, k, 0).wait()

    own_same(0)

    @pl.when(inner)
    def _():
        own_same(1)
        own_same(2)

    @pl.loop(0, count)
    def _(n):
        chunk = lax.rem(me + n, count)
        ours = lax.rem(n, group) == 0

        @pl.when(jnp.logical_not((n == 0) | (inner & ours & (chunk // places == other))))
        def _():
            take_same(chunk)

        place(1, chunk, side * half_rows)

    @pl.when(upper)
    def _():
        cross_local(line, col).wait()
        place(0, me, 0)

        @pl.loop(1, count)
        def _(n):
            chunk = lax.rem(me + n, count)
            remote(
                far_pairs.at[0], got.at[0, chunk], cross_send.at[0], cross_recv.at[chunk], row, col
            ).wait_recv()
            place(0, chunk, 0)

    @pl.when(upper & inner)
    def _():
        pass_sent()

    for to in near_order:
        main_copy(to).wait_send()

    @pl.when(inner)
    def _():
        for to_seat in seats[1:]:
            for z in range(2):
                near_copy(to_seat, z).wait_send()

    @pl.when(outer)
    def _():
        for to_seat in seats:
            for z in range(2):
                near_copy(to_seat, z).wait_send()


    for k in range(half_rows):
        for h in range(cols):

            @pl.when(spot != k * cols + h)
            def _():
                same_copy(0, k, h).wait_send()

                @pl.when(inner)
                def _():
                    same_copy(1, k, h).wait_send()
                    same_copy(2, k, h).wait_send()

            @pl.when(me != (half_rows + k) * cols + h)
            def _():
                cross_copy(k, h).wait_send()


def exchange_form(rows, cols, spectra, window_flags):
    bands, windows, parts, chans, bins = spectra.shape
    count = rows * cols
    places = count // 2
    half_rows, group = rows // 2, places // 2
    height = chans * parts * windows
    dma = pltpu.SemaphoreType.DMA
    shape = (bands, 2, 1, rows * chans, cols * chans, bins)
    return pl.pallas_call(
        functools.partial(main_kernel, rows, cols),
        out_shape=jax.ShapeDtypeStruct(shape, jnp.float32),
        in_specs=[
            pl.BlockSpec(memory_space=pltpu.HBM),
            pl.BlockSpec(memory_space=pltpu.HBM),
        ],
        out_specs=pl.BlockSpec(memory_space=pltpu.VMEM),
        scratch_shapes=[
            pltpu.VMEM(spectra.shape, spectra.dtype),
            pltpu.VMEM((chans, windows), window_flags.dtype),
            pltpu.VMEM((parts, bins // LANES, windows * chans, LANES), jnp.float32),
            pltpu.VMEM((bands, group, 2, height, LANES), jnp.bfloat16),
            pltpu.VMEM((count, height, LANES), jnp.bfloat16),
            pltpu.VMEM((places, 2, height, LANES), jnp.bfloat16),
            pltpu.VMEM(((count + places * 2) * chans, parts, windows, LANES), jnp.float32),
            pltpu.VMEM((2, count, half_rows, 16, LANES), jnp.bfloat16),
            pltpu.VMEM((places, half_rows, 16, LANES), jnp.bfloat16),
            pltpu.VMEM((3, places, half_rows, 16, LANES), jnp.bfloat16),
            pltpu.SemaphoreType.REGULAR((count,)),
            pltpu.SemaphoreType.REGULAR,
            dma((3,)),
            dma((places,)),
            dma((count,)),
            dma((count,)),
            dma((places,)),
            dma((count,)),
            dma((places,)),
            dma((count,)),
            dma,
            dma((3, places)),
            dma((count,)),
            dma((3,)),
        ],
        compiler_params=pltpu.CompilerParams(
            collective_id=0, has_side_effects=True, vmem_limit_bytes=24 * 1024 * 1024
        ),
    )(
        pltpu.with_memory_space_constraint(spectra, pltpu.HBM),
        pltpu.with_memory_space_constraint(jnp.transpose(window_flags), pltpu.HBM),
    )


def solution(mesh):
    rows, cols = mesh.shape["row"], mesh.shape["col"]

    def on_device(spectra, window_flags):
        bands, windows, _, chans, bins = spectra.shape
        fits = (
            bands == 2
            and rows % 4 == 0
            and 2 * bins == rows * cols * LANES
            and bins % (2 * LANES) == 0
            and chans == 2
            and cols == 2
            and windows == 32
        )
        if fits:
            return exchange_form(rows, cols, spectra, window_flags)
        return gather_form(spectra, window_flags)

    in_specs = (P("parts", None, None, ("row", "col"), None), P("parts", ("row", "col")))
    out_specs = P("parts", None, "col", None, "row", None)
    return jax.shard_map(
        on_device, mesh=mesh, in_specs=in_specs, out_specs=out_specs, check_vma=False
    )
```

```python
import functools

import jax
import jax.numpy as jnp
from jax import lax
from jax.experimental import pallas as pl
from jax.experimental.pallas import tpu as pltpu
from jax.sharding import PartitionSpec as P

HALFWIN = 64
LANES = 128
epsilon = 1e-06


def window_mean(magnitude):
    bins = magnitude.shape[-1]
    positions = jnp.arange(bins, dtype=jnp.int32)
    near = (jnp.abs(positions[:, None] - positions[None, :]) <= HALFWIN).astype(jnp.float32)
    total = jnp.einsum("...g,gf->...f", magnitude, near, precision=lax.Precision.HIGHEST)
    counted = (
        jnp.minimum(positions + HALFWIN, bins - 1) - jnp.maximum(positions - HALFWIN, 0) + 1
    ).astype(jnp.float32)
    return total / counted


def whiten(values):
    magnitude = jnp.sqrt(values[:, :, 0] * values[:, :, 0] + values[:, :, 1] * values[:, :, 1])
    smooth = window_mean(magnitude)
    return (values / (smooth[:, :, None] + epsilon)).astype(jnp.bfloat16)


def combine_parts(prods, keep):
    real_part = prods[..., 0, 0, :, :, :] + prods[..., 1, 1, :, :, :]
    imag_part = prods[..., 1, 0, :, :, :] - prods[..., 0, 1, :, :, :]
    return jnp.stack([real_part * keep, imag_part * keep], axis=-4)


def gather_form(spectra, window_flags):
    per_device = spectra.shape[3]
    flag_values = window_flags.astype(jnp.float32)[None, :, None, :, None]
    payload = whiten(spectra.astype(jnp.float32) * flag_values)
    row_index = lax.axis_index("row")
    col_index = lax.axis_index("col")
    col_count = lax.axis_size("col")
    row_count = lax.axis_size("row")
    half_size = row_count * per_device
    cols_here = col_count * per_device
    slot = jnp.arange(half_size, dtype=jnp.int32)
    first = (slot // per_device * col_count + col_index) * per_device + slot % per_device
    second = row_index * cols_here + jnp.arange(cols_here, dtype=jnp.int32)
    keep = (first[:, None] <= second[None, :]).astype(jnp.float32)[:, :, None]
    pieces = []
    for band_index in range(spectra.shape[0]):
        first_rows = lax.all_gather(payload[band_index : band_index + 1], "row", axis=3, tiled=True)
        second_rows = lax.all_gather(
            payload[band_index : band_index + 1], "col", axis=3, tiled=True
        )
        prods = jnp.einsum(
            "wpif,wqjf->pqijf", first_rows[0], second_rows[0], preferred_element_type=jnp.float32
        )
        pieces.append(combine_parts(prods, keep))
    result = jnp.stack(pieces, axis=0)
    return result[:, :, None]


def spread_band(x_ref, flag_ref, rows_ref, b):
    _, windows, parts, chans, _ = x_ref.shape
    for w in range(windows):
        for p in range(parts):
            pair = x_ref[b, w, p].astype(jnp.float32)
            for n in range(rows_ref.shape[1]):
                rows_ref[p, n, pl.ds(w * chans, chans)] = pair[:, n * LANES : (n + 1) * LANES]
    extent = (windows, windows)
    same = lax.broadcasted_iota(jnp.int32, extent, 0) == lax.broadcasted_iota(jnp.int32, extent, 1)
    flags = flag_ref[...].astype(jnp.float32)
    return [
        jnp.sum(jnp.where(same, flags[c : c + 1], 0.0), axis=1, keepdims=True)
        for c in range(chans)
    ]


def whiten_band(x_ref, flag_ref, rows_ref, y_ref, b):
    _, windows, _, chans, bins = x_ref.shape
    flags = spread_band(x_ref, flag_ref, rows_ref, b)
    step = 2 * LANES
    chunks, group = bins // LANES, y_ref.shape[1]
    near = lax.broadcasted_iota(jnp.int32, (2 * step, step), 0) - LANES
    here = lax.broadcasted_iota(jnp.int32, (2 * step, step), 1)
    inside = (jnp.abs(near - here) <= HALFWIN).astype(jnp.float32).astype(jnp.bfloat16)
    mags = []
    for c in range(chans):
        picked = pl.ds(c, windows, stride=chans)
        line = []
        for n in range(chunks):
            re = rows_ref[0, n, picked] * flags[c]
            im = rows_ref[1, n, picked] * flags[c]
            line.append(jnp.sqrt(re * re + im * im))
        mags.append(jnp.concatenate(line, axis=1))
    mag = jnp.concatenate(mags, axis=0)
    high = mag.astype(jnp.bfloat16)
    low = (mag - high.astype(jnp.float32)).astype(jnp.bfloat16)
    for at in range(0, bins, step):
        start, stop = max(at - LANES, 0), min(at + step + LANES, bins)
        near_rows = inside[start - at + LANES : stop - at + LANES]
        total = jnp.dot(
            high[:, start:stop], near_rows, preferred_element_type=jnp.float32
        ) + jnp.dot(low[:, start:stop], near_rows, preferred_element_type=jnp.float32)
        spot = at + lax.broadcasted_iota(jnp.int32, (1, step), 1)
        counted = (
            jnp.minimum(spot + HALFWIN, bins - 1) - jnp.maximum(spot - HALFWIN, 0) + 1
        ).astype(jnp.float32)
        scale = 1.0 / (total / counted + epsilon)
        for c in range(chans):
            picked = pl.ds(c, windows, stride=chans)
            for p in range(2):
                for half in range(2):
                    lanes = slice(half * LANES, (half + 1) * LANES)
                    value = rows_ref[p, at // LANES + half, picked] * flags[c]
                    out = value * scale[c * windows : (c + 1) * windows, lanes]
                    chunk = at // LANES + half
                    y_ref[
                        b, chunk % group, chunk // group, pl.ds((c * 2 + p) * windows, windows)
                    ] = out.astype(jnp.bfloat16)


def fold(values):
    index = lax.broadcasted_iota(jnp.int32, values[0].shape, 0)
    shift = 1
    while len(values) > 1:
        even = lax.rem(index // shift, 2) == 0
        paired = []
        for n in range(0, len(values), 2):
            u, v = values[n], values[n + 1]
            moved = pltpu.roll(jnp.where(even, v, u), 8 - shift, 0)
            paired.append(jnp.where(even, u, v) + moved)
        values = paired
        shift *= 2
    return values[0]


def by_eight(values):
    total = values[0:8]
    for at in range(8, values.shape[0], 8):
        total = total + values[at : at + 8]
    return total


def block(wide_ref, first, second, cols):
    out = []
    for h in range(cols):
        reals, imags = [], []
        for k in range(2):
            re_a, im_a = wide_ref[first + h * 2 + k, 0], wide_ref[first + h * 2 + k, 1]
            for n in range(cols * 2):
                re_j, im_j = wide_ref[second + n, 0], wide_ref[second + n, 1]
                reals.append(by_eight(re_a * re_j + im_a * im_j))
                imags.append(by_eight(im_a * re_j - re_a * im_j))
        out.append(jnp.concatenate([fold(reals), fold(imags)], axis=0).astype(jnp.bfloat16))
    return out


def main_kernel(
    rows, cols, raw_ref, raw_flags, out_ref, x_ref, flag_ref, spread, sent, held, near_held, wide,
    got, far_pairs, near_pairs, here_sem, go_sem, in_sem, main_send, far_recv, pass_send,
    near_send, near_recv, cross_send, cross_recv, cross_own, same_send, same_recv, same_own,
):
    count, half_rows, plane_rows = rows * cols, rows // 2, rows // 4
    places, group = half_rows * cols, plane_rows * cols
    per_row = cols * 2
    windows = x_ref.shape[1]
    row, col = lax.axis_index("row"), lax.axis_index("col")
    me = row * cols + col
    side, line = row // half_rows, lax.rem(row, half_rows)
    spot = line * cols + col
    other = 1 - side
    plane, seat = line // plane_rows, lax.rem(spot, group)
    inner, outer = plane == other, plane == side
    upper, lower = side == 1, side == 0

    def remote(src, dst, send_sem, recv_sem, to_row, to_col):
        return pltpu.make_async_remote_copy(
            src_ref=src,
            dst_ref=dst,
            send_sem=send_sem,
            recv_sem=recv_sem,
            device_id={"row": to_row, "col": to_col},
            device_id_type=pl.DeviceIdType.MESH,
        )

    def signal(sem, peer):
        pl.semaphore_signal(
            sem,
            inc=1,
            device_id={"row": peer // cols, "col": lax.rem(peer, cols)},
            device_id_type=pl.DeviceIdType.MESH,
        )

    flag_load = pltpu.make_async_copy(raw_flags, flag_ref, in_sem.at[2])
    flag_load.start()
    loads = []
    for n, b in enumerate((other, side)):
        loads.append(pltpu.make_async_copy(raw_ref.at[b], x_ref.at[b], in_sem.at[n]))
        loads[n].start()
    def turn_of(peer):
        return peer // cols * cols + cols - 1 - lax.rem(peer, cols)

    barrier = pltpu.get_barrier_semaphore()
    for k in range(1, count):
        peer = lax.rem(me + k, count)

        @pl.when(turn_of(peer) > turn_of(me))
        def _():
            signal(barrier, peer)

    @pl.when(turn_of(me) > 0)
    def _():
        pl.semaphore_wait(barrier, turn_of(me))

    for k in range(count):
        peer = lax.rem(row * cols + cols - 1 + count - k, count)

        @pl.when(turn_of(peer) < turn_of(me))
        def _():
            signal(here_sem.at[me], peer)

    def ready(peer):
        @pl.when(turn_of(peer) > turn_of(me))
        def _():
            pl.semaphore_wait(here_sem.at[peer], 1)

    def pass_copy(source, z, src):
        return remote(
            src, held.at[side * places + source], pass_send.at[source * 2 + z],
            far_recv.at[side * places + source],
            other * half_rows + z * plane_rows + seat // cols, col,
        )

    def near_copy(to_seat, z):
        return remote(
            sent.at[other, to_seat, z], near_held.at[spot, z], near_send.at[to_seat * 2 + z],
            near_recv.at[spot * 2 + z],
            side * half_rows + other * plane_rows + to_seat // cols, lax.rem(to_seat, cols),
        )

    def main_copy(to):
        return remote(
            sent.at[side, lax.rem(to, group), to // group], held.at[me], main_send.at[to],
            far_recv.at[me], side * half_rows + to // cols, lax.rem(to, cols),
        )

    seats = [
        lax.rem(line + i, plane_rows) * cols + lax.rem(col + j, cols)
        for i in range(plane_rows)
        for j in range(cols)
    ]
    near_order = [
        (to_plane * group + to_seat) for to_plane in (plane, 1 - plane) for to_seat in seats
    ][1:]

    def send_near(to_seats):
        for to_seat in to_seats:
            ready(side * places + other * group + to_seat)
            for z in range(2):
                near_copy(to_seat, z).start()

    def sent_near(to_seats):
        for to_seat in to_seats:
            for z in range(2):
                near_copy(to_seat, z).wait_send()

    def send_own(z):
        ready(other * places + z * group + seat)
        pass_copy(spot, z, sent.at[other, seat, z]).start()

    flag_load.wait()
    loads[0].wait()
    whiten_band(x_ref, flag_ref, spread, sent, other)

    @pl.when(inner)
    def _():
        send_near(seats[1:])
        send_own(side)

    @pl.when(outer)
    def _():
        send_near(seats[:2])

    loads[1].wait()
    whiten_band(x_ref, flag_ref, spread, sent, side)
    @pl.when(outer)
    def _():
        for n in range(2, group):
            sent_near(seats[n - 2 : n - 1])
            send_near(seats[n : n + 1])

    for n, to in enumerate(near_order):

        @pl.when(to // group == side)
        def _():
            ready(side * places + to)

        if n == group - 1:

            @pl.when(outer)
            def _():
                sent_near(seats[group - 2 :])

        main_copy(to).start()

    @pl.when(inner)
    def _():
        send_own(other)

    def widen(slot, base):
        for c in range(2):
            for p in range(2):
                wide[base + c, p] = slot[pl.ds((c * 2 + p) * windows, windows)].astype(jnp.float32)

    def take(n):
        remote(
            sent.at[0, 0, 0], held.at[n], main_send.at[0], far_recv.at[n], row, col
        ).wait_recv()
        widen(held.at[n], n * 2)

    def take_near(source, z):
        remote(
            sent.at[0, 0, 0], near_held.at[source, z], near_send.at[0],
            near_recv.at[source * 2 + z], row, col,
        ).wait_recv()

    def widen_near(source, ref, z):
        widen(ref.at[z], (count + z * places + source) * 2)

    near_sources = [other * group + n for n in seats[1:]] + [side * group + n for n in seats]

    @pl.when(inner)
    def _():
        for source in near_sources:
            for z in range(2):
                take_near(source, z)
                pass_copy(source, z, near_held.at[source, z]).start()
                widen_near(source, near_held.at[source], z)

    def chunk_of(kind):
        return me if kind == 0 else other * places + (kind - 1) * group + seat

    def same_copy(kind, k, h):
        to, chunk = k * cols + h, chunk_of(kind)
        return remote(
            near_pairs.at[kind, to, pl.ds(0, k + 1)], got.at[1, chunk, pl.ds(0, k + 1)],
            same_send.at[kind, to], same_recv.at[chunk], side * half_rows + k, h,
        )

    def same_local(kind, k, h):
        to, chunk = k * cols + h, chunk_of(kind)
        return pltpu.make_async_copy(
            near_pairs.at[kind, to, pl.ds(0, k + 1)], got.at[1, chunk, pl.ds(0, k + 1)],
            same_own.at[kind],
        )

    def same(kind, base):
        @pl.loop(0, half_rows)
        def _(step):
            r = lax.rem(line + 1 + step, half_rows)

            @pl.loop(0, r + 1)
            def _(q):
                found = block(wide, base + q * per_row, base + r * per_row, cols)
                for h in range(cols):
                    near_pairs[kind, r * cols + h, q] = found[h]

            for k in range(half_rows):

                @pl.when(r == k)
                def _():
                    for h in range(cols):

                        @pl.when(spot != k * cols + h)
                        def _():
                            same_copy(kind, k, h).start()

                        @pl.when(spot == k * cols + h)
                        def _():
                            same_local(kind, k, h).start()

    def cross_copy(r, h):
        return remote(
            far_pairs.at[r * cols + h], got.at[0, me], cross_send.at[r * cols + h],
            cross_recv.at[me], half_rows + r, h,
        )

    def cross_local(r, h):
        return pltpu.make_async_copy(far_pairs.at[r * cols + h], got.at[0, me], cross_own)

    @pl.when(lower)
    def _():
        for b in range(2):
            for p in range(2):
                out_ref[b, p, 0, half_rows * 2 :] = jnp.zeros(
                    (half_rows * 2,) + out_ref.shape[4:], jnp.float32
                )

    @pl.when(inner)
    def _():
        for z in range(2):
            widen_near(spot, sent.at[other, seat], z)
        for z in range(2):
            same(1 + z, (count + z * places) * 2)

    widen(sent.at[side, seat, plane], me * 2)

    @pl.loop(1, places)
    def _(n):
        take(side * places + lax.rem(spot + n, places))

    same(0, side * places * 2)

    for n in range(places):

        @pl.when(outer | (n % group != seat))
        def _():
            ready(other * places + n)

    def pass_sent():
        for source in [spot] + near_sources:
            for z in range(2):
                pass_copy(source, z, near_held.at[0, 0]).wait_send()

    @pl.loop(0, half_rows)
    def _(step):
        turn = jnp.where(lower, step // 2, half_rows // 2 - 1 - step // 2)
        line_far = 2 * turn + lax.rem(row + step, 2)
        row_far = other * half_rows + line_far
        for h in range(cols):
            take(row_far * cols + h)

        @pl.loop(0, half_rows)
        def _(j):
            q = side * line_far + other * j
            r = side * j + other * line_far
            found = block(wide, q * per_row, (half_rows + r) * per_row, cols)
            for h in range(cols):
                far_pairs[r * cols + h, q] = found[h]

        @pl.when(lower & inner & (step == 0))
        def _():
            pass_sent()
            signal(go_sem, side * places + side * group + seat)

        @pl.when(lower & outer & (step == 0))
        def _():
            pl.semaphore_wait(go_sem, 1)

        @pl.when(lower)
        def _():
            for h in range(cols):
                cross_copy(line_far, h).start()

    @pl.when(upper)
    def _():
        for to in near_order[::-1]:
            cross_copy(to // cols, lax.rem(to, cols)).start()
        cross_local(line, col).start()

    index = lax.broadcasted_iota(jnp.int32, (8, LANES), 0)
    second = row * per_row + lax.rem(index, per_row)

    def place(kind, chunk, at_row):
        b, lanes = chunk // places, lax.rem(chunk, places) * LANES
        for q in range(half_rows):
            keep = (at_row + q) * per_row + col * 2 + index // per_row <= second
            pair = got[kind, chunk, q].astype(jnp.float32)
            for p in range(2):
                value = jnp.where(keep, pair[p * 8 : p * 8 + 8], 0.0)
                for k in range(2):
                    out_ref[
                        b, p, 0, (at_row + q) * 2 + k, :, pl.ds(pl.multiple_of(lanes, LANES), LANES)
                    ] = value[k * per_row : (k + 1) * per_row]

    def take_same(chunk):
        for k in range(half_rows):

            @pl.when(line == k)
            def _():
                remote(
                    near_pairs.at[0, 0, pl.ds(0, k + 1)], got.at[1, chunk, pl.ds(0, k + 1)],
                    same_send.at[0, 0], same_recv.at[chunk], row, col,
                ).wait_recv()

    def own_same(kind):
        for k in range(half_rows):

            @pl.when(line == k)
            def _():
                same_local(kind, k, 0).wait()

    own_same(0)

    @pl.when(inner)
    def _():
        own_same(1)
        own_same(2)

    @pl.loop(0, count)
    def _(n):
        chunk = lax.rem(me + n, count)
        ours = lax.rem(n, group) == 0

        @pl.when(jnp.logical_not((n == 0) | (inner & ours & (chunk // places == other))))
        def _():
            take_same(chunk)

        place(1, chunk, side * half_rows)

    for to in near_order:
        main_copy(to).wait_send()

    @pl.when(inner)
    def _():
        for to_seat in seats[1:]:
            for z in range(2):
                near_copy(to_seat, z).wait_send()


    for k in range(half_rows):
        for h in range(cols):

            @pl.when(spot != k * cols + h)
            def _():
                same_copy(0, k, h).wait_send()

                @pl.when(inner)
                def _():
                    same_copy(1, k, h).wait_send()
                    same_copy(2, k, h).wait_send()

            @pl.when(me != (half_rows + k) * cols + h)
            def _():
                cross_copy(k, h).wait_send()

    @pl.when(upper)
    def _():
        cross_local(line, col).wait()
        place(0, me, 0)

        @pl.loop(1, count)
        def _(n):
            chunk = lax.rem(me + n, count)
            remote(
                far_pairs.at[0], got.at[0, chunk], cross_send.at[0], cross_recv.at[chunk], row, col
            ).wait_recv()
            place(0, chunk, 0)

    @pl.when(upper & inner)
    def _():
        pass_sent()


def exchange_form(rows, cols, spectra, window_flags):
    bands, windows, parts, chans, bins = spectra.shape
    count = rows * cols
    places = count // 2
    half_rows, group = rows // 2, places // 2
    height = chans * parts * windows
    dma = pltpu.SemaphoreType.DMA
    shape = (bands, 2, 1, rows * chans, cols * chans, bins)
    return pl.pallas_call(
        functools.partial(main_kernel, rows, cols),
        out_shape=jax.ShapeDtypeStruct(shape, jnp.float32),
        in_specs=[
            pl.BlockSpec(memory_space=pltpu.HBM),
            pl.BlockSpec(memory_space=pltpu.HBM),
        ],
        out_specs=pl.BlockSpec(memory_space=pltpu.VMEM),
        scratch_shapes=[
            pltpu.VMEM(spectra.shape, spectra.dtype),
            pltpu.VMEM((chans, windows), window_flags.dtype),
            pltpu.VMEM((parts, bins // LANES, windows * chans, LANES), jnp.float32),
            pltpu.VMEM((bands, group, 2, height, LANES), jnp.bfloat16),
            pltpu.VMEM((count, height, LANES), jnp.bfloat16),
            pltpu.VMEM((places, 2, height, LANES), jnp.bfloat16),
            pltpu.VMEM(((count + places * 2) * chans, parts, windows, LANES), jnp.float32),
            pltpu.VMEM((2, count, half_rows, 16, LANES), jnp.bfloat16),
            pltpu.VMEM((places, half_rows, 16, LANES), jnp.bfloat16),
            pltpu.VMEM((3, places, half_rows, 16, LANES), jnp.bfloat16),
            pltpu.SemaphoreType.REGULAR((count,)),
            pltpu.SemaphoreType.REGULAR,
            dma((3,)),
            dma((places,)),
            dma((count,)),
            dma((count,)),
            dma((places,)),
            dma((count,)),
            dma((places,)),
            dma((count,)),
            dma,
            dma((3, places)),
            dma((count,)),
            dma((3,)),
        ],
        compiler_params=pltpu.CompilerParams(
            collective_id=0, has_side_effects=True, vmem_limit_bytes=24 * 1024 * 1024
        ),
    )(
        pltpu.with_memory_space_constraint(spectra, pltpu.HBM),
        pltpu.with_memory_space_constraint(jnp.transpose(window_flags), pltpu.HBM),
    )


def solution(mesh):
    rows, cols = mesh.shape["row"], mesh.shape["col"]

    def on_device(spectra, window_flags):
        bands, windows, _, chans, bins = spectra.shape
        fits = (
            bands == 2
            and rows % 4 == 0
            and 2 * bins == rows * cols * LANES
            and bins % (2 * LANES) == 0
            and chans == 2
            and cols == 2
            and windows == 32
        )
        if fits:
            return exchange_form(rows, cols, spectra, window_flags)
        return gather_form(spectra, window_flags)

    in_specs = (P("parts", None, None, ("row", "col"), None), P("parts", ("row", "col")))
    out_specs = P("parts", None, "col", None, "row", None)
    return jax.shard_map(
        on_device, mesh=mesh, in_specs=in_specs, out_specs=out_specs, check_vma=False
    )
```

```python
import functools

import jax
import jax.numpy as jnp
from jax import lax
from jax.experimental import pallas as pl
from jax.experimental.pallas import tpu as pltpu
from jax.sharding import PartitionSpec as P

HALFWIN = 64
LANES = 128
epsilon = 1e-06


def window_mean(magnitude):
    bins = magnitude.shape[-1]
    positions = jnp.arange(bins, dtype=jnp.int32)
    near = (jnp.abs(positions[:, None] - positions[None, :]) <= HALFWIN).astype(jnp.float32)
    total = jnp.einsum("...g,gf->...f", magnitude, near, precision=lax.Precision.HIGHEST)
    counted = (
        jnp.minimum(positions + HALFWIN, bins - 1) - jnp.maximum(positions - HALFWIN, 0) + 1
    ).astype(jnp.float32)
    return total / counted


def whiten(values):
    magnitude = jnp.sqrt(values[:, :, 0] * values[:, :, 0] + values[:, :, 1] * values[:, :, 1])
    smooth = window_mean(magnitude)
    return (values / (smooth[:, :, None] + epsilon)).astype(jnp.bfloat16)


def combine_parts(prods, keep):
    real_part = prods[..., 0, 0, :, :, :] + prods[..., 1, 1, :, :, :]
    imag_part = prods[..., 1, 0, :, :, :] - prods[..., 0, 1, :, :, :]
    return jnp.stack([real_part * keep, imag_part * keep], axis=-4)


def gather_form(spectra, window_flags):
    per_device = spectra.shape[3]
    flag_values = window_flags.astype(jnp.float32)[None, :, None, :, None]
    payload = whiten(spectra.astype(jnp.float32) * flag_values)
    row_index = lax.axis_index("row")
    col_index = lax.axis_index("col")
    col_count = lax.axis_size("col")
    row_count = lax.axis_size("row")
    half_size = row_count * per_device
    cols_here = col_count * per_device
    slot = jnp.arange(half_size, dtype=jnp.int32)
    first = (slot // per_device * col_count + col_index) * per_device + slot % per_device
    second = row_index * cols_here + jnp.arange(cols_here, dtype=jnp.int32)
    keep = (first[:, None] <= second[None, :]).astype(jnp.float32)[:, :, None]
    pieces = []
    for band_index in range(spectra.shape[0]):
        first_rows = lax.all_gather(payload[band_index : band_index + 1], "row", axis=3, tiled=True)
        second_rows = lax.all_gather(
            payload[band_index : band_index + 1], "col", axis=3, tiled=True
        )
        prods = jnp.einsum(
            "wpif,wqjf->pqijf", first_rows[0], second_rows[0], preferred_element_type=jnp.float32
        )
        pieces.append(combine_parts(prods, keep))
    result = jnp.stack(pieces, axis=0)
    return result[:, :, None]


def spread_band(x_ref, flag_ref, rows_ref, b):
    _, windows, parts, chans, _ = x_ref.shape
    for w in range(windows):
        for p in range(parts):
            pair = x_ref[b, w, p].astype(jnp.float32)
            for n in range(rows_ref.shape[1]):
                rows_ref[p, n, pl.ds(w * chans, chans)] = pair[:, n * LANES : (n + 1) * LANES]
    extent = (windows, windows)
    same = lax.broadcasted_iota(jnp.int32, extent, 0) == lax.broadcasted_iota(jnp.int32, extent, 1)
    flags = flag_ref[...].astype(jnp.float32)
    return [
        jnp.sum(jnp.where(same, flags[c : c + 1], 0.0), axis=1, keepdims=True)
        for c in range(chans)
    ]


def whiten_band(x_ref, flag_ref, rows_ref, y_ref, b):
    _, windows, _, chans, bins = x_ref.shape
    flags = spread_band(x_ref, flag_ref, rows_ref, b)
    step = 2 * LANES
    chunks, group = bins // LANES, y_ref.shape[1]
    near = lax.broadcasted_iota(jnp.int32, (2 * step, step), 0) - LANES
    here = lax.broadcasted_iota(jnp.int32, (2 * step, step), 1)
    inside = (jnp.abs(near - here) <= HALFWIN).astype(jnp.float32).astype(jnp.bfloat16)
    mags = []
    for c in range(chans):
        picked = pl.ds(c, windows, stride=chans)
        line = []
        for n in range(chunks):
            re = rows_ref[0, n, picked] * flags[c]
            im = rows_ref[1, n, picked] * flags[c]
            line.append(jnp.sqrt(re * re + im * im))
        mags.append(jnp.concatenate(line, axis=1))
    mag = jnp.concatenate(mags, axis=0)
    high = mag.astype(jnp.bfloat16)
    low = (mag - high.astype(jnp.float32)).astype(jnp.bfloat16)
    for at in range(0, bins, step):
        start, stop = max(at - LANES, 0), min(at + step + LANES, bins)
        near_rows = inside[start - at + LANES : stop - at + LANES]
        total = jnp.dot(
            high[:, start:stop], near_rows, preferred_element_type=jnp.float32
        ) + jnp.dot(low[:, start:stop], near_rows, preferred_element_type=jnp.float32)
        spot = at + lax.broadcasted_iota(jnp.int32, (1, step), 1)
        counted = (
            jnp.minimum(spot + HALFWIN, bins - 1) - jnp.maximum(spot - HALFWIN, 0) + 1
        ).astype(jnp.float32)
        scale = 1.0 / (total / counted + epsilon)
        for c in range(chans):
            picked = pl.ds(c, windows, stride=chans)
            for p in range(2):
                for half in range(2):
                    lanes = slice(half * LANES, (half + 1) * LANES)
                    value = rows_ref[p, at // LANES + half, picked] * flags[c]
                    out = value * scale[c * windows : (c + 1) * windows, lanes]
                    chunk = at // LANES + half
                    y_ref[
                        b, chunk % group, chunk // group, pl.ds((c * 2 + p) * windows, windows)
                    ] = out.astype(jnp.bfloat16)


def fold(values):
    index = lax.broadcasted_iota(jnp.int32, values[0].shape, 0)
    shift = 1
    while len(values) > 1:
        even = lax.rem(index // shift, 2) == 0
        paired = []
        for n in range(0, len(values), 2):
            u, v = values[n], values[n + 1]
            moved = pltpu.roll(jnp.where(even, v, u), 8 - shift, 0)
            paired.append(jnp.where(even, u, v) + moved)
        values = paired
        shift *= 2
    return values[0]


def by_eight(values):
    total = values[0:8]
    for at in range(8, values.shape[0], 8):
        total = total + values[at : at + 8]
    return total


def block(wide_ref, first, second, cols):
    out = []
    for h in range(cols):
        reals, imags = [], []
        for k in range(2):
            re_a, im_a = wide_ref[first + h * 2 + k, 0], wide_ref[first + h * 2 + k, 1]
            for n in range(cols * 2):
                re_j, im_j = wide_ref[second + n, 0], wide_ref[second + n, 1]
                reals.append(by_eight(re_a * re_j + im_a * im_j))
                imags.append(by_eight(im_a * re_j - re_a * im_j))
        out.append(jnp.concatenate([fold(reals), fold(imags)], axis=0).astype(jnp.bfloat16))
    return out


def main_kernel(
    rows, cols, raw_ref, raw_flags, out_ref, x_ref, flag_ref, spread, sent, held, near_held, wide,
    got, far_pairs, near_pairs, here_sem, go_sem, in_sem, main_send, far_recv, pass_send,
    near_send, near_recv, cross_send, cross_recv, cross_own, same_send, same_recv, same_own,
):
    count, half_rows, plane_rows = rows * cols, rows // 2, rows // 4
    places, group = half_rows * cols, plane_rows * cols
    per_row = cols * 2
    windows = x_ref.shape[1]
    row, col = lax.axis_index("row"), lax.axis_index("col")
    me = row * cols + col
    side, line = row // half_rows, lax.rem(row, half_rows)
    spot = line * cols + col
    other = 1 - side
    plane, seat = line // plane_rows, lax.rem(spot, group)
    inner, outer = plane == other, plane == side
    upper, lower = side == 1, side == 0

    def remote(src, dst, send_sem, recv_sem, to_row, to_col):
        return pltpu.make_async_remote_copy(
            src_ref=src,
            dst_ref=dst,
            send_sem=send_sem,
            recv_sem=recv_sem,
            device_id={"row": to_row, "col": to_col},
            device_id_type=pl.DeviceIdType.MESH,
        )

    def signal(sem, to_row, to_col):
        pl.semaphore_signal(
            sem,
            inc=1,
            device_id={"row": to_row, "col": to_col},
            device_id_type=pl.DeviceIdType.MESH,
        )

    flag_load = pltpu.make_async_copy(raw_flags, flag_ref, in_sem.at[2])
    flag_load.start()
    loads = []
    for n, b in enumerate((other, side)):
        loads.append(pltpu.make_async_copy(raw_ref.at[b], x_ref.at[b], in_sem.at[n]))
        loads[n].start()
    def turn_of(peer):
        return peer // cols * cols + cols - 1 - lax.rem(peer, cols)

    my_turn = turn_of(me)
    others = sorted(range(count), key=lambda n: n // cols * cols + cols - 1 - n % cols)
    barrier = pltpu.get_barrier_semaphore()
    for turn, peer in enumerate(others):

        @pl.when(my_turn < turn)
        def _():
            signal(barrier, peer // cols, peer % cols)

    @pl.when(my_turn > 0)
    def _():
        pl.semaphore_wait(barrier, my_turn)

    for turn, peer in reversed(list(enumerate(others))):

        @pl.when(my_turn > turn)
        def _():
            signal(here_sem.at[me], peer // cols, peer % cols)

    def ready(peer):
        @pl.when(turn_of(peer) > my_turn)
        def _():
            pl.semaphore_wait(here_sem.at[peer], 1)

    def pass_copy(source, z, src):
        return remote(
            src, held.at[side * places + source], pass_send.at[source * 2 + z],
            far_recv.at[side * places + source],
            other * half_rows + z * plane_rows + seat // cols, col,
        )

    def near_copy(to_seat, z):
        return remote(
            sent.at[other, to_seat, z], near_held.at[spot, z], near_send.at[to_seat * 2 + z],
            near_recv.at[spot * 2 + z],
            side * half_rows + other * plane_rows + to_seat // cols, lax.rem(to_seat, cols),
        )

    def main_copy(to):
        return remote(
            sent.at[side, lax.rem(to, group), to // group], held.at[me], main_send.at[to],
            far_recv.at[me], side * half_rows + to // cols, lax.rem(to, cols),
        )

    seats = [
        lax.rem(line + i, plane_rows) * cols + lax.rem(col + j, cols)
        for i in range(plane_rows)
        for j in range(cols)
    ]
    near_order = [
        (to_plane * group + to_seat) for to_plane in (plane, 1 - plane) for to_seat in seats
    ][1:]

    def send_near(to_seats):
        for to_seat in to_seats:
            ready(side * places + other * group + to_seat)
            for z in (other, side):
                near_copy(to_seat, z).start()

    def sent_near(to_seats):
        for to_seat in to_seats:
            for z in range(2):
                near_copy(to_seat, z).wait_send()

    def send_own(z):
        ready(other * places + z * group + seat)
        pass_copy(spot, z, sent.at[other, seat, z]).start()

    flag_load.wait()
    loads[0].wait()
    whiten_band(x_ref, flag_ref, spread, sent, other)

    @pl.when(inner)
    def _():
        send_near(seats[1:])
        send_own(side)

    @pl.when(outer)
    def _():
        send_near(seats[:2])

    loads[1].wait()
    whiten_band(x_ref, flag_ref, spread, sent, side)
    @pl.when(outer)
    def _():
        for n in range(2, group):
            sent_near(seats[n - 2 : n - 1])
            send_near(seats[n : n + 1])

    for n, to in enumerate(near_order):

        @pl.when(to // group == side)
        def _():
            ready(side * places + to)

        if n == group - 1:

            @pl.when(outer)
            def _():
                sent_near(seats[group - 2 :])

        main_copy(to).start()

    @pl.when(inner)
    def _():
        send_own(other)

    def widen(slot, base):
        for c in range(2):
            for p in range(2):
                wide[base + c, p] = slot[pl.ds((c * 2 + p) * windows, windows)].astype(jnp.float32)

    def take(n):
        remote(
            sent.at[0, 0, 0], held.at[n], main_send.at[0], far_recv.at[n], row, col
        ).wait_recv()
        widen(held.at[n], n * 2)

    def take_near(source, z):
        remote(
            sent.at[0, 0, 0], near_held.at[source, z], near_send.at[0],
            near_recv.at[source * 2 + z], row, col,
        ).wait_recv()

    def widen_near(source, ref, z):
        widen(ref.at[z], (count + z * places + source) * 2)

    near_sources = [other * group + n for n in seats[1:]] + [side * group + n for n in seats]

    @pl.when(inner)
    def _():
        for source in near_sources:
            for z in (other, side):
                take_near(source, z)
                pass_copy(source, z, near_held.at[source, z]).start()
                widen_near(source, near_held.at[source], z)

    def chunk_of(kind):
        return me if kind == 0 else other * places + (kind - 1) * group + seat

    def same_copy(kind, k, h):
        to, chunk = k * cols + h, chunk_of(kind)
        return remote(
            near_pairs.at[kind, to, pl.ds(0, k + 1)], got.at[1, chunk, pl.ds(0, k + 1)],
            same_send.at[kind, to], same_recv.at[chunk], side * half_rows + k, h,
        )

    def same_local(kind, k, h):
        to, chunk = k * cols + h, chunk_of(kind)
        return pltpu.make_async_copy(
            near_pairs.at[kind, to, pl.ds(0, k + 1)], got.at[1, chunk, pl.ds(0, k + 1)],
            same_own.at[kind],
        )

    def same(kind, base):
        @pl.loop(0, half_rows)
        def _(step):
            r = lax.rem((1 - plane) * plane_rows + step, half_rows)

            @pl.loop(0, r + 1)
            def _(q):
                found = block(wide, base + q * per_row, base + r * per_row, cols)
                for h in range(cols):
                    near_pairs[kind, r * cols + h, q] = found[h]

            for k in range(half_rows):

                @pl.when(r == k)
                def _():
                    for h in range(cols):

                        @pl.when(spot != k * cols + h)
                        def _():
                            same_copy(kind, k, h).start()

                        @pl.when(spot == k * cols + h)
                        def _():
                            same_local(kind, k, h).start()

    def cross_copy(r, h):
        return remote(
            far_pairs.at[r * cols + h], got.at[0, me], cross_send.at[r * cols + h],
            cross_recv.at[me], half_rows + r, h,
        )

    def cross_local(r, h):
        return pltpu.make_async_copy(far_pairs.at[r * cols + h], got.at[0, me], cross_own)

    @pl.when(lower)
    def _():
        for b in range(2):
            for p in range(2):
                out_ref[b, p, 0, half_rows * 2 :] = jnp.zeros(
                    (half_rows * 2,) + out_ref.shape[4:], jnp.float32
                )

    @pl.when(inner)
    def _():
        for z in range(2):
            widen_near(spot, sent.at[other, seat], z)
        for z in range(2):
            same(1 + z, (count + z * places) * 2)

    widen(sent.at[side, seat, plane], me * 2)

    @pl.loop(1, places)
    def _(n):
        take(side * places + lax.rem(spot + n, places))

    same(0, side * places * 2)

    for n in range(places):

        @pl.when(outer | (n % group != seat))
        def _():
            ready(other * places + n)

    def pass_sent():
        for source in [spot] + near_sources:
            for z in range(2):
                pass_copy(source, z, near_held.at[0, 0]).wait_send()

    @pl.loop(0, half_rows)
    def _(step):
        turn = jnp.where(lower, step // 2, half_rows // 2 - 1 - step // 2)
        line_far = 2 * turn + lax.rem(row + step, 2)
        row_far = other * half_rows + line_far
        for h in range(cols):
            take(row_far * cols + h)

        @pl.loop(0, half_rows)
        def _(j):
            q = side * line_far + other * j
            r = side * j + other * line_far
            found = block(wide, q * per_row, (half_rows + r) * per_row, cols)
            for h in range(cols):
                far_pairs[r * cols + h, q] = found[h]

        @pl.when(lower & outer & (step == 0))
        def _():
            pl.semaphore_wait(go_sem, 1)

        @pl.when(lower)
        def _():
            for h in range(cols):
                cross_copy(line_far, h).start()

        @pl.when(lower & inner & (step == 1))
        def _():
            pass_sent()
            signal(go_sem, side * half_rows + side * plane_rows + lax.div(seat, cols), col)

    @pl.when(upper)
    def _():
        for to in near_order[::-1]:
            cross_copy(to // cols, lax.rem(to, cols)).start()
        cross_local(line, col).start()

    index = lax.broadcasted_iota(jnp.int32, (8, LANES), 0)
    second = row * per_row + lax.rem(index, per_row)

    def place(kind, chunk, at_row):
        b, lanes = chunk // places, lax.rem(chunk, places) * LANES
        for q in range(half_rows):
            keep = (at_row + q) * per_row + col * 2 + index // per_row <= second
            pair = got[kind, chunk, q].astype(jnp.float32)
            for p in range(2):
                value = jnp.where(keep, pair[p * 8 : p * 8 + 8], 0.0)
                for k in range(2):
                    out_ref[
                        b, p, 0, (at_row + q) * 2 + k, :, pl.ds(pl.multiple_of(lanes, LANES), LANES)
                    ] = value[k * per_row : (k + 1) * per_row]

    def take_same(chunk):
        for k in range(half_rows):

            @pl.when(line == k)
            def _():
                remote(
                    near_pairs.at[0, 0, pl.ds(0, k + 1)], got.at[1, chunk, pl.ds(0, k + 1)],
                    same_send.at[0, 0], same_recv.at[chunk], row, col,
                ).wait_recv()

    def own_same(kind):
        for k in range(half_rows):

            @pl.when(line == k)
            def _():
                same_local(kind, k, 0).wait()

    own_same(0)

    @pl.when(inner)
    def _():
        own_same(1)
        own_same(2)

    @pl.loop(0, count)
    def _(n):
        chunk = lax.rem(me + n, count)
        ours = lax.rem(n, group) == 0

        @pl.when(jnp.logical_not((n == 0) | (inner & ours & (chunk // places == other))))
        def _():
            take_same(chunk)

        place(1, chunk, side * half_rows)

    for to in near_order:
        main_copy(to).wait_send()

    @pl.when(inner)
    def _():
        for to_seat in seats[1:]:
            for z in range(2):
                near_copy(to_seat, z).wait_send()


    for k in range(half_rows):
        for h in range(cols):

            @pl.when(spot != k * cols + h)
            def _():
                same_copy(0, k, h).wait_send()

                @pl.when(inner)
                def _():
                    same_copy(1, k, h).wait_send()
                    same_copy(2, k, h).wait_send()

            @pl.when(me != (half_rows + k) * cols + h)
            def _():
                cross_copy(k, h).wait_send()

    @pl.when(upper)
    def _():
        cross_local(line, col).wait()
        place(0, me, 0)

        @pl.loop(1, count)
        def _(n):
            chunk = lax.rem(me + n, count)
            remote(
                far_pairs.at[0], got.at[0, chunk], cross_send.at[0], cross_recv.at[chunk], row, col
            ).wait_recv()
            place(0, chunk, 0)

    @pl.when(upper & inner)
    def _():
        pass_sent()


def exchange_form(rows, cols, spectra, window_flags):
    bands, windows, parts, chans, bins = spectra.shape
    count = rows * cols
    places = count // 2
    half_rows, group = rows // 2, places // 2
    height = chans * parts * windows
    dma = pltpu.SemaphoreType.DMA
    shape = (bands, 2, 1, rows * chans, cols * chans, bins)
    return pl.pallas_call(
        functools.partial(main_kernel, rows, cols),
        out_shape=jax.ShapeDtypeStruct(shape, jnp.float32),
        in_specs=[
            pl.BlockSpec(memory_space=pltpu.HBM),
            pl.BlockSpec(memory_space=pltpu.HBM),
        ],
        out_specs=pl.BlockSpec(memory_space=pltpu.VMEM),
        scratch_shapes=[
            pltpu.VMEM(spectra.shape, spectra.dtype),
            pltpu.VMEM((chans, windows), window_flags.dtype),
            pltpu.VMEM((parts, bins // LANES, windows * chans, LANES), jnp.float32),
            pltpu.VMEM((bands, group, 2, height, LANES), jnp.bfloat16),
            pltpu.VMEM((count, height, LANES), jnp.bfloat16),
            pltpu.VMEM((places, 2, height, LANES), jnp.bfloat16),
            pltpu.VMEM(((count + places * 2) * chans, parts, windows, LANES), jnp.float32),
            pltpu.VMEM((2, count, half_rows, 16, LANES), jnp.bfloat16),
            pltpu.VMEM((places, half_rows, 16, LANES), jnp.bfloat16),
            pltpu.VMEM((3, places, half_rows, 16, LANES), jnp.bfloat16),
            pltpu.SemaphoreType.REGULAR((count,)),
            pltpu.SemaphoreType.REGULAR,
            dma((3,)),
            dma((places,)),
            dma((count,)),
            dma((count,)),
            dma((places,)),
            dma((count,)),
            dma((places,)),
            dma((count,)),
            dma,
            dma((3, places)),
            dma((count,)),
            dma((3,)),
        ],
        compiler_params=pltpu.CompilerParams(
            collective_id=0, has_side_effects=True, vmem_limit_bytes=24 * 1024 * 1024
        ),
    )(
        pltpu.with_memory_space_constraint(spectra, pltpu.HBM),
        pltpu.with_memory_space_constraint(jnp.transpose(window_flags), pltpu.HBM),
    )


def solution(mesh):
    rows, cols = mesh.shape["row"], mesh.shape["col"]

    def on_device(spectra, window_flags):
        bands, windows, _, chans, bins = spectra.shape
        fits = (
            bands == 2
            and rows % 4 == 0
            and 2 * bins == rows * cols * LANES
            and bins % (2 * LANES) == 0
            and chans == 2
            and cols == 2
            and windows == 32
        )
        if fits:
            return exchange_form(rows, cols, spectra, window_flags)
        return gather_form(spectra, window_flags)

    in_specs = (P("parts", None, None, ("row", "col"), None), P("parts", ("row", "col")))
    out_specs = P("parts", None, "col", None, "row", None)
    return jax.shard_map(
        on_device, mesh=mesh, in_specs=in_specs, out_specs=out_specs, check_vma=False
    )
```
